256 devices in a mesh: heads: 8 (over x, y_lo), tok: 32 (over z, y_hi, core).
Axes of the slice: x: 4, y: 4 (y_hi: 2, y_lo: 2; y = y_hi * 2 + y_lo), z: 8, core: 2. Of those that a mesh axis runs over, the one named last changes fastest.
Arguments:
- queries: bfloat16 [32, 16, 32, 1024], P('tok', None, None, 'heads'), may hold values from -12 to 12
- key_rows: bfloat16 [32, 16, 32, 1024], P('tok', None, None, 'heads'), may hold values from -6 to 6
- value_rows: bfloat16 [32, 16, 32, 1024], P('tok', None, None, 'heads'), may hold values from -6 to 6
- residual: bfloat16 [16, 32, 32, 1024], P('heads', 'tok'), may hold values from -3 to 3
- w_out: bfloat16 [1024, 1024], P('heads'), may hold values from -0.375 to 0.375
- w_neck: bfloat16 [1024, 256], replicated, may hold values from -0.1875 to 0.1875
- w_first: bfloat16 [3, 3, 3, 256, 256], replicated, may hold values from -0.109375 to 0.109375
- w_second: bfloat16 [3, 3, 3, 256, 256], replicated, may hold values from -0.109375 to 0.109375
- w_class: bfloat16 [256], replicated, may hold values from -0.5 to 0.5
- labels: int32 [16, 32, 32], P('heads', None, 'tok'), may hold values from 0 to 1, as said below
Outputs:
- encoded: bfloat16 [16, 32, 32, 1024], P('heads', 'tok')
- dice_loss: float32 [], replicated
- grad_encoded: bfloat16 [16, 32, 32, 1024], P('heads', 'tok')
The draws below stay inside these ranges and needn't reach their ends.
Inputs may be any that keep to these rules, and one draw needn't show every extreme that they name: `labels`: 1 marks a fault cell.
All inputs are finite; a program needn't handle non-finite values.
Results may differ from the reference program's by a relative error of at most 0.025.
Values may be sent and summed in bfloat16 or wider, within the bound.
A program may use at most 128 MiB of HBM per device.

```python
import jax
import jax.numpy as jnp
from jax import lax

D = 1024
HEADS = 16
HD = 64
C = 256
NC = 16
NT = 32
NI = 32
TOKENS = 16384


def query_key_pair(key):
    base = jax.random.fold_in(key, 4242)
    key_query, key_keys = jax.random.split(base, 2)
    width = HEADS * HD
    query_draw = jnp.clip(2.5 * jax.random.normal(key_query, (TOKENS, width), jnp.float32), -12.0, 12.0)
    keys_draw = jnp.clip(jax.random.normal(key_keys, (TOKENS, width), jnp.float32), -6.0, 6.0)
    return (query_draw.reshape(NT, NC, NI, width), keys_draw.reshape(NT, NC, NI, width))


def draw_queries(key, part):
    return query_key_pair(key)[0].astype(jnp.bfloat16)


def draw_key_rows(key, part):
    return query_key_pair(key)[1].astype(jnp.bfloat16)


def draw_labels(key, part):
    cross_pos = jnp.arange(NC, dtype=jnp.int32)[:, None, None]
    inline_pos = jnp.arange(NI, dtype=jnp.int32)[None, None, :]
    span_inline = max(NI - 1, 1)
    span_cross = max(NC - 1, 1)
    threshold = 60 * (span_inline + 2 * inline_pos) * (span_cross + 2 * cross_pos) // (span_inline * span_cross)
    uniform_ints = jax.random.randint(jax.random.fold_in(key, 777), (NC, NT, NI), 0, 1000, dtype=jnp.int32)
    return (uniform_ints < threshold).astype(jnp.int32)


def steps_of(rng, shape, pieces, smallest, top_value):
    def one(dim, parts):
        draws = jax.random.uniform(jax.random.fold_in(jax.random.fold_in(rng, 6), dim), (parts,), jnp.float32, smallest / len(pieces), top_value / len(pieces))
        return jnp.repeat(jnp.exp(draws), shape[dim] // parts).reshape((-1,) + (1,) * (len(shape) - dim - 1))

    factor_of = one(*pieces[0])
    for cut in pieces[1:]:
        factor_of = factor_of * one(*cut)
    return factor_of


def gaussian(own_key, shape, scale, bound, shards=(), held_as=jnp.bfloat16):
    result = jax.random.normal(own_key, shape, jnp.float32) * scale
    if len(shards) > 0:
        result = steps_of(own_key, shape, shards, -0.22, 0.18) * result
    return jnp.clip(result, min=-bound, max=bound).astype(held_as)


def setup_inputs(seed: int = 0) -> dict:
    arg_keys = jax.random.split(jax.random.key(seed), 11)
    return {
        "queries": draw_queries(jax.random.fold_in(arg_keys[10], 71), 0),
        "key_rows": draw_key_rows(jax.random.fold_in(arg_keys[10], 71), 0),
        "value_rows": gaussian(arg_keys[2], (NT, NC, NI, HEADS * HD), 1.0, 6.0, ((0, 32), (3, 8))),
        "residual": gaussian(arg_keys[3], (NC, NT, NI, D), 0.5, 3.0, ((0, 8), (1, 32))),
        "w_out": gaussian(arg_keys[4], (HEADS * HD, D), (HEADS * HD // 4) ** -0.5, 0.375, ((0, 8),)),
        "w_neck": gaussian(arg_keys[5], (D, C), D ** -0.5, 0.1875),
        "w_first": gaussian(arg_keys[6], (3, 3, 3, C, C), (27 * C // 2) ** -0.5, 0.109375),
        "w_second": gaussian(arg_keys[7], (3, 3, 3, C, C), (27 * C // 2) ** -0.5, 0.109375),
        "w_class": gaussian(arg_keys[8], (C,), (C // 2) ** -0.5, 0.5),
        "labels": draw_labels(jax.random.fold_in(arg_keys[10], 71), 0),
    }


OFFSETS = [(along_c, along_t, along_x) for along_c in range(3) for along_t in range(3) for along_x in range(3)]
LOSS_SCALE = 64.0


def silu_slope(volume):
    sigma = jax.nn.sigmoid(volume)
    return sigma * (1.0 + volume * (1.0 - sigma))


def conv_apply(volume, weights, flipped):
    padded = jnp.pad(volume, ((1, 1), (1, 1), (1, 1), (0, 0)))
    extent = volume.shape
    outputs = jnp.zeros(extent[:3] + (weights.shape[3],), jnp.float32)
    for (along_c, along_t, along_x) in OFFSETS:
        if flipped:
            anchor = (2 - along_c, 2 - along_t, 2 - along_x)
            matrix = jnp.transpose(weights[along_c, along_t, along_x])
        else:
            anchor = (along_c, along_t, along_x)
            matrix = weights[along_c, along_t, along_x]
        window = padded[anchor[0]:anchor[0] + extent[0], anchor[1]:anchor[1] + extent[1], anchor[2]:anchor[2] + extent[2]]
        product = jnp.dot(window.reshape(-1, extent[3]), matrix, preferred_element_type=jnp.float32)
        outputs = outputs + product.reshape(outputs.shape)
    return outputs


def attend_block(query_block, keys_wide, values_wide):
    scores = jnp.einsum('qhd,khd->hqk', query_block.astype(jnp.float32), keys_wide) * (HD ** -0.5)
    row_peak = jnp.max(scores, axis=-1, keepdims=True)
    raw_weights = jnp.exp(scores - row_peak)
    totals = jnp.sum(raw_weights, axis=-1)
    mixing = raw_weights.astype(jnp.bfloat16)
    mixed = jnp.einsum('hqk,khd->qhd', mixing.astype(jnp.float32), values_wide)
    return (mixed / jnp.transpose(totals)[:, :, None]).astype(jnp.bfloat16)


def reference(queries, key_rows, value_rows, residual, w_out, w_neck, w_first, w_second, w_class, labels):
    width = HEADS * HD
    keys_wide = key_rows.reshape(TOKENS, HEADS, HD).astype(jnp.float32)
    values_wide = value_rows.reshape(TOKENS, HEADS, HD).astype(jnp.float32)
    block_rows = 256 if TOKENS % 256 == 0 else TOKENS
    query_blocks = queries.reshape(TOKENS // block_rows, block_rows, HEADS, HD)
    attended = lax.map(lambda query_block: attend_block(query_block, keys_wide, values_wide), query_blocks)
    attended = attended.reshape(NT, NC, NI, width)
    attention_out = jnp.einsum('tzxe,ed->ztxd', attended.astype(jnp.float32), w_out.astype(jnp.float32))
    encoded = (residual.astype(jnp.float32) + attention_out).astype(jnp.bfloat16)
    neck_feats = jnp.einsum('ztxd,dc->ztxc', encoded.astype(jnp.float32), w_neck.astype(jnp.float32)).astype(jnp.bfloat16)
    hidden_one = conv_apply(neck_feats, w_first, False)
    active_one = jax.nn.silu(hidden_one).astype(jnp.bfloat16)
    hidden_two = conv_apply(active_one, w_second, False)
    active_two = jax.nn.silu(hidden_two).astype(jnp.bfloat16)
    logits = jnp.einsum('ztxc,c->ztx', active_two.astype(jnp.float32), w_class.astype(jnp.float32))
    probability = jax.nn.sigmoid(logits)
    fault_mask = labels.astype(jnp.float32)
    intersection = jnp.sum(probability * fault_mask)
    dice_denominator = jnp.sum(probability) + jnp.sum(fault_mask)
    dice_loss = 1.0 - 2.0 * intersection / dice_denominator
    grad_logits = LOSS_SCALE * TOKENS * (-2.0) * (fault_mask * dice_denominator - intersection) / (dice_denominator * dice_denominator) * probability * (1.0 - probability)
    grad_hidden_two = (grad_logits[..., None] * w_class.astype(jnp.float32) * silu_slope(hidden_two)).astype(jnp.bfloat16)
    grad_active_one = conv_apply(grad_hidden_two, w_second, True)
    grad_hidden_one = (grad_active_one * silu_slope(hidden_one)).astype(jnp.bfloat16)
    grad_neck = conv_apply(grad_hidden_one, w_first, True).astype(jnp.bfloat16)
    grad_encoded = jnp.einsum('ztxc,dc->ztxd', grad_neck.astype(jnp.float32), w_neck.astype(jnp.float32)).astype(jnp.bfloat16)
    return (encoded, dice_loss, grad_encoded)
```

```python
import functools

import jax
import jax.numpy as jnp
from jax import lax
from jax.experimental import pallas as pl
from jax.experimental.pallas import tpu as pltpu
from jax.sharding import PartitionSpec as P

MESH = pl.DeviceIdType.MESH
BF = jnp.bfloat16
F32 = jnp.float32
HD = 64
LOSS_SCALE = 64.0
LOG2E = 1.4426950408889634
NN = (((1,), (0,)), ((), ()))
NT = (((1,), (1,)), ((), ()))
TOK = 512
ROWS = 528
NZ = 8
SLOT = {(0, 0): 0, (0, 1): 1}
for _k in (1, 2, 3):
    _b = 4 * _k - 2
    SLOT.update({(-_k, 0): _b, (_k, 0): _b + 1, (-_k, 1): _b + 2, (_k, 1): _b + 3})
SLOT.update({(4, 0): 14, (4, 1): 15})
DISTANCE = [None] * 16
for _key, _slot in SLOT.items():
    DISTANCE[_slot] = _key
TILES = [(0, 1), (2, 3, 4, 5), (6, 7, 8, 9), (10, 11, 12, 13), (14, 15)]


def place():
    heads, tok = lax.axis_index("heads"), lax.axis_index("tok")
    return heads, tok, tok // 4, (tok // 2) % 2, tok % 2


def at(heads, tok):
    return {"heads": heads, "tok": tok}


def attention_kernel(
    q_hbm, k_hbm, v_hbm, lab_hbm, w_hbm,
    out_ref, lab_out, w_full,
    kv, q_buf, qx, acc, peak, o_send, o_recv, lse_send, lse_recv, lab_send, lab_recv, w_buf,
    local_sem, kv_send, kv_recv, mate_send, y_send, y_recv, w_send, w_recv,
):
    heads, tok, z, y, core = place()
    up = at(heads, (tok + 4) % (4 * NZ))
    down = at(heads, (tok + 4 * NZ - 4) % (4 * NZ))
    mate = at(heads, tok + 1 - 2 * core)
    across = at(heads, tok + 2 - 4 * y)
    others = [at((heads + d) % 8, tok) for d in range(1, 8)]

    local = [
        pltpu.make_async_copy(k_hbm, kv.at[0, 0:TOK, 0:128], local_sem.at[0]),
        pltpu.make_async_copy(v_hbm, kv.at[0, 0:TOK, 128:256], local_sem.at[1]),
        pltpu.make_async_copy(lab_hbm, kv.at[0, TOK:ROWS, :], local_sem.at[2]),
        pltpu.make_async_copy(q_hbm, q_buf.at[0], local_sem.at[3]),
        pltpu.make_async_copy(w_hbm, w_buf, local_sem.at[4]),
    ]
    for copy in local:
        copy.start()
    barrier = pltpu.get_barrier_semaphore()
    peers = [up, down, mate, across] + others
    for peer in peers:
        pl.semaphore_signal(barrier, inc=1, device_id=peer, device_id_type=MESH)
    pl.semaphore_wait(barrier, len(peers))
    for copy in local:
        copy.wait()

    sent = []

    def send(src, dst, send_sem, recv_sem, peer):
        copy = pltpu.make_async_remote_copy(
            src_ref=src, dst_ref=dst, send_sem=send_sem, recv_sem=recv_sem, device_id=peer, device_id_type=MESH
        )
        copy.start()
        sent.append(copy)
        return copy

    arrivals = {}
    n_ring = [0]

    def pass_on(distance):
        slot = SLOT[(distance, 0)]
        src = kv.at[slot]

        def ring(to, peer, rows, part):
            dst = SLOT[(to, 0)]
            lo, hi = rows
            copy = send(
                kv.at[slot, lo:hi], kv.at[dst, lo:hi], kv_send.at[n_ring[0]], kv_recv.at[16 * part + dst], peer
            )
            n_ring[0] += 1
            arrivals.setdefault((to, 0), []).append(copy)

        whole = (0, ROWS)
        if distance <= 0 and distance > -3:
            ring(distance - 1, up, whole, 0)
        if distance >= 0 and distance < 3:
            ring(distance + 1, down, whole, 0)
        if distance == -3:
            ring(4, up, (0, 256), 0)
        if distance == 3:
            ring(4, down, (256, ROWS), 1)
        dst = SLOT[(distance, 1)]
        copy = send(src, kv.at[dst], mate_send.at[slot], kv_recv.at[dst], mate)
        arrivals.setdefault((distance, 1), []).append(copy)

    def await_block(key):
        for copy in arrivals[key]:
            copy.wait_recv()

    def prepare(half):
        lane = lax.broadcasted_iota(jnp.int32, (TOK, 128), 1)
        q = q_buf[half].astype(F32) * (HD**-0.5 * LOG2E)
        high = q.astype(BF)
        low = (q - high.astype(F32)).astype(BF)
        zero = jnp.zeros_like(high)
        rows = slice(half * TOK, (half + 1) * TOK)
        for h in range(2):
            mine = (lane < HD) if h == 0 else (lane >= HD)
            qx[h, rows, 0:128] = jnp.where(mine, high, zero)
            qx[h, rows, 128:256] = jnp.where(mine, low, zero)
        acc[rows] = jnp.zeros((TOK, 256), F32)
        peak[:, rows] = jnp.full((2, TOK, 128), -1e30, F32)

    def attend(first, count, slots):
        def body(half, carry):
            rows = pl.ds(pl.multiple_of(half * TOK, TOK), TOK)
            lane = lax.broadcasted_iota(jnp.int32, (TOK, 128), 1)
            k = jnp.concatenate([kv[s, 0:TOK, 0:128] for s in slots], axis=0)
            kk = jnp.concatenate([k, k], axis=1)
            v = jnp.concatenate([kv[s, 0:TOK, 128:256] for s in slots], axis=0)
            vx = jnp.concatenate([v, jnp.ones_like(v)], axis=1)
            scores = [lax.dot_general(qx[h, rows, :], kk, NT, preferred_element_type=F32) for h in range(2)]
            sums, factors = [], []
            for h in range(2):
                old = peak[h, rows, :]
                new = jnp.maximum(old, jnp.max(scores[h], axis=1, keepdims=True))
                peak[h, rows, :] = new
                factors.append(jnp.exp2(old - new))
                mixing = jnp.exp2(scores[h] - new[:, :1]).astype(BF)
                sums.append(lax.dot_general(mixing, vx, NN, preferred_element_type=F32))
            factor = jnp.where(lane < HD, factors[0], factors[1])
            for part in (slice(0, 128), slice(128, 256)):
                acc[rows, part] = acc[rows, part] * factor + jnp.where(lane < HD, sums[0][:, part], sums[1][:, part])
            return carry

        lax.fori_loop(first, first + count, body, 0)

    def finish(half):
        lane = lax.broadcasted_iota(jnp.int32, (TOK, 128), 1)
        rows = slice(half * TOK, (half + 1) * TOK)
        total = acc[rows, 128:256]
        top = jnp.where(lane < HD, peak[0, rows], peak[1, rows])
        return acc[rows, 0:128] / total, top + jnp.log(total) * LOG2E

    pass_on(0)
    q_copy = send(q_buf.at[0], q_buf.at[1], y_send.at[0], y_recv.at[0], across)
    prepare(0)
    await_block((0, 1))
    attend(0, 1, TILES[0])
    q_copy.wait_recv()
    prepare(1)
    attend(1, 1, TILES[0])

    my_rows = w_full.at[pl.ds(pl.multiple_of(heads * 128, 128), 128), :]
    own_w = pltpu.make_async_copy(w_buf, my_rows, local_sem.at[5])
    own_w.start()
    w_copies = [send(w_buf, my_rows, w_send.at[d], w_recv.at[d], others[d]) for d in range(7)]

    for k in (1, 2, 3):
        for distance in (-k, k):
            await_block((distance, 0))
            pass_on(distance)
        for distance in (-k, k):
            await_block((distance, 1))
        if k < 3:
            attend(0, 2, TILES[k])
    attend(1, 1, TILES[3])
    await_block((4, 0))
    mate_slot = SLOT[(4, 1)]
    last = send(kv.at[SLOT[(4, 0)]], kv.at[mate_slot], mate_send.at[14], kv_recv.at[mate_slot], mate)
    last.wait_recv()
    attend(1, 1, TILES[4])

    part, lse = finish(1)
    o_send[...] = part.astype(BF)
    flat = lse.T
    lse_send[0:8] = flat[0:8]
    lse_send[8:16] = flat[64:72]
    label_rows = jnp.concatenate([kv[s, TOK:ROWS, :] for s in range(16)], axis=0)
    row = lax.broadcasted_iota(jnp.int32, (64, 256), 0)
    col = lax.broadcasted_iota(jnp.int32, (64, 256), 1)
    pick = jnp.zeros((64, 256), jnp.bool_)
    for s, (distance, other) in enumerate(DISTANCE):
        owner_core = core if other == 0 else 1 - core
        owner = ((z + distance + NZ) % NZ) * 4 + y * 2 + owner_core
        pick = pick | (((row % 32) == owner) & (col == 16 * s + row // 32))
    by_depth = lax.dot_general(
        jnp.where(pick, 1.0, 0.0).astype(BF), label_rows, NN, preferred_element_type=F32
    )
    tok_across = tok + 2 - 4 * y
    lane64 = lax.broadcasted_iota(jnp.int32, (64, 256), 1)

    def at_depth(depth):
        chosen = jnp.sum(jnp.where(lane64 == depth, by_depth, 0.0), axis=1, keepdims=True)
        return jnp.broadcast_to(chosen, (64, 128))

    lab_send[...] = at_depth(tok_across)
    o_copy = send(o_send, o_recv, y_send.at[1], y_recv.at[1], across)
    lse_copy = send(lse_send, lse_recv, y_send.at[2], y_recv.at[2], across)
    lab_copy = send(lab_send, lab_recv, y_send.at[3], y_recv.at[3], across)
    attend(0, 1, TILES[3])
    attend(0, 1, TILES[4])
    mine, my_lse = finish(0)
    o_copy.wait_recv()
    lse_copy.wait_recv()
    lab_copy.wait_recv()
    head0 = jnp.broadcast_to(lse_recv[0:1], (64, TOK))
    head1 = jnp.broadcast_to(lse_recv[8:9], (64, TOK))
    its_lse = jnp.concatenate([head0, head1], axis=0).T
    top = jnp.maximum(my_lse, its_lse)
    my_share, its_share = jnp.exp2(my_lse - top), jnp.exp2(its_lse - top)
    merged = (my_share * mine + its_share * o_recv[...].astype(F32)) / (my_share + its_share)
    out_ref[...] = merged.astype(BF)
    lab_out[...] = at_depth(tok) + lab_recv[...]
    own_w.wait()
    for copy in w_copies:
        copy.wait_recv()
    for copy in sent:
        copy.wait_send()


def attention(queries, key_rows, value_rows, label_rows, w_out):
    dma = pltpu.SemaphoreType.DMA
    return pl.pallas_call(
        attention_kernel,
        out_shape=(
            jax.ShapeDtypeStruct((TOK, 128), BF),
            jax.ShapeDtypeStruct((64, 128), F32),
            jax.ShapeDtypeStruct((1024, 1024), BF),
        ),
        in_specs=[pl.BlockSpec(memory_space=pl.ANY)] * 5,
        out_specs=(
            pl.BlockSpec(memory_space=pltpu.VMEM),
            pl.BlockSpec(memory_space=pltpu.VMEM),
            pl.BlockSpec(memory_space=pl.ANY),
        ),
        scratch_shapes=[
            pltpu.VMEM((16, ROWS, 256), BF),
            pltpu.VMEM((2, TOK, 128), BF),
            pltpu.VMEM((2, 2 * TOK, 256), BF),
            pltpu.VMEM((2 * TOK, 256), F32),
            pltpu.VMEM((2, 2 * TOK, 128), F32),
            pltpu.VMEM((TOK, 128), BF),
            pltpu.VMEM((TOK, 128), BF),
            pltpu.VMEM((16, TOK), F32),
            pltpu.VMEM((16, TOK), F32),
            pltpu.VMEM((64, 128), F32),
            pltpu.VMEM((64, 128), F32),
            pltpu.VMEM((128, 1024), BF),
            dma((6,)),
            dma((8,)),
            dma((32,)),
            dma((16,)),
            dma((4,)),
            dma((4,)),
            dma((7,)),
            dma((7,)),
        ],
        compiler_params=pltpu.CompilerParams(
            collective_id=0, has_side_effects=True, vmem_limit_bytes=58 << 20
        ),
        name="attention",
    )(queries, key_rows, value_rows, label_rows, w_out)


NEAR = [(dh, dt) for dh in (-1, 0, 1) for dt in (-1, 0, 1) if (dh, dt) != (0, 0)]


def decoder_kernel(
    att_ref, lab_ref, wf_hbm, res_ref, neck_hbm, first_hbm, second_hbm, class_ref,
    enc_ref, loss_ref, grad_ref,
    att_all, wf, neck, first, second, halo_one, halo_two, halo_three, halo_four, grad_two,
    stat_a, stat_b, send_a, send_b,
    local_sem, a_send, a_recv, h_send, h_recv, s_send, s_recv, r_send, r_recv,
):
    heads, tok, z, y, core = place()
    loads = [
        pltpu.make_async_copy(src, dst, local_sem.at[i])
        for i, (src, dst) in enumerate(
            ((wf_hbm, wf), (neck_hbm, neck), (first_hbm, first), (second_hbm, second))
        )
    ]
    mine = pl.ds(pl.multiple_of(heads * 128, 128), 128)
    own_rows = pl.ds(pl.multiple_of(heads * 64, 64), 64)
    own = pltpu.make_async_copy(att_ref.at[own_rows], att_all.at[:, mine], local_sem.at[4])
    own.start()
    for load in loads:
        load.start()

    by_head = [at((heads + d) % 8, tok) for d in range(1, 8)]
    near = [at((heads + dh + 8) % 8, (tok + dt + 32) % 32) for dh, dt in NEAR]
    group_a = [
        at((heads + d // 2) % 8, tok if d % 2 == 0 else tok + 1 - 2 * core) for d in range(1, 16)
    ]
    group_b = [
        at(heads, (tok + 4 * (d // 2)) % 32 if d % 2 == 0 else (tok + 4 * (d // 2) + 2 - 4 * y + 32) % 32)
        for d in range(1, 16)
    ]
    peers = by_head + near + group_a + group_b
    barrier = pltpu.get_barrier_semaphore()
    for peer in peers:
        pl.semaphore_signal(barrier, inc=1, device_id=peer, device_id_type=MESH)
    pl.semaphore_wait(barrier, len(peers))

    sent = []

    def send(src, dst, send_sem, recv_sem, peer):
        copy = pltpu.make_async_remote_copy(
            src_ref=src, dst_ref=dst, send_sem=send_sem, recv_sem=recv_sem, device_id=peer, device_id_type=MESH
        )
        copy.start()
        sent.append(copy)
        return copy

    copies = []
    for i in range(7):
        theirs = lax.rem(heads + i + 1, 8)
        copies.append(
            send(
                att_ref.at[pl.ds(pl.multiple_of(theirs * 64, 64), 64)],
                att_all.at[:, mine],
                a_send.at[i],
                a_recv.at[i],
                by_head[i],
            )
        )

    def start_halo(stage, halo):
        halves = []
        for i, (dh, dt) in enumerate(NEAR):
            src, dst = {0: ((32, 96), (32, 96)), 1: ((64, 96), (0, 32)), -1: ((32, 64), (96, 128))}[dh]
            halves.append(
                send(
                    halo.at[1, src[0] : src[1]],
                    halo.at[1 - dt, dst[0] : dst[1]],
                    h_send.at[stage, i],
                    h_recv.at[stage, i],
                    near[i],
                )
            )
        return halves

    def end_halo(halo, halves):
        width = halo.shape[2]
        for copy in halves:
            copy.wait_recv()

        @pl.when(heads == 0)
        def _():
            halo[:, 0:32] = jnp.zeros((3, 32, width), BF)

        @pl.when(heads == 7)
        def _():
            halo[:, 96:128] = jnp.zeros((3, 32, width), BF)

        @pl.when(tok == 0)
        def _():
            halo[0] = jnp.zeros((128, width), BF)

        @pl.when(tok == 31)
        def _():
            halo[2] = jnp.zeros((128, width), BF)

    inline = lax.broadcasted_iota(jnp.int32, (64, 256), 0) % 32

    def conv(halo, weights, flipped):
        parts = []
        for e in range(3):
            total = None
            for a in range(3):
                for b in range(3):
                    c, t = (2 - a, 2 - b) if flipped else (a, b)
                    term = lax.dot_general(
                        halo[t, 32 * c : 32 * c + 64],
                        weights[(a * 3 + b) * 3 + e],
                        NT if flipped else NN,
                        preferred_element_type=F32,
                    )
                    total = term if total is None else total + term
            parts.append(total)
        if flipped:
            parts = parts[::-1]
        before = jnp.where(inline == 0, 0.0, pltpu.roll(parts[0], 1, 0))
        after = jnp.where(inline == 31, 0.0, pltpu.roll(parts[2], 63, 0))
        return before + parts[1] + after

    def sigmoid(v):
        return 1.0 / (1.0 + jnp.exp(-v))

    own.wait()
    loads[0].wait()
    loads[1].wait()
    for copy in copies:
        copy.wait_recv()
    projected = lax.dot_general(att_all[...], wf[...], NN, preferred_element_type=F32)
    encoded = (res_ref[...].astype(F32) + projected).astype(BF)
    enc_ref[...] = encoded
    halo_one[1, 32:96] = lax.dot_general(encoded, neck[...], NN, preferred_element_type=F32).astype(BF)
    halves = start_halo(0, halo_one)
    loads[2].wait()
    end_halo(halo_one, halves)
    hidden_one = conv(halo_one, first, False)
    gate_one = sigmoid(hidden_one)
    halo_two[1, 32:96] = (hidden_one * gate_one).astype(BF)
    halves = start_halo(1, halo_two)
    slope_one = gate_one * (1.0 + hidden_one * (1.0 - gate_one))
    loads[3].wait()
    end_halo(halo_two, halves)
    hidden_two = conv(halo_two, second, False)
    gate_two = sigmoid(hidden_two)
    active_two = (hidden_two * gate_two).astype(BF).astype(F32)
    w_class = class_ref[0:1].astype(F32)
    logits = jnp.sum(active_two * w_class, axis=1, keepdims=True)
    probability = jnp.broadcast_to(sigmoid(logits), (64, 128))
    labels = lab_ref[...]

    def over_cells(value):
        return jnp.sum(value, axis=0, keepdims=True)

    row8 = lax.broadcasted_iota(jnp.int32, (8, 128), 0)
    stats = jnp.where(
        row8 == 0,
        over_cells(probability * labels),
        jnp.where(row8 == 1, over_cells(probability), over_cells(labels)),
    )
    index_a = heads * 2 + core
    send_a[...] = stats
    stat_copies = [
        send(send_a, stat_a.at[index_a], s_send.at[d], s_recv.at[d], group_a[d]) for d in range(15)
    ]
    stat_a[index_a] = stats
    spread = probability * (1.0 - probability)
    slope_two = gate_two * (1.0 + hidden_two * (1.0 - gate_two))
    unscaled = jnp.concatenate([spread, spread], axis=1) * w_class * slope_two
    halo_three[1, 32:96, 0:256] = unscaled.astype(BF)
    halo_three[1, 32:96, 256:384] = labels.astype(BF)
    halves = start_halo(2, halo_three)
    for copy in stat_copies:
        copy.wait_recv()
    partial = stat_a[0]
    for i in range(1, 16):
        partial = partial + stat_a[i]
    index_b = z * 2 + y
    send_b[...] = partial
    stat_copies = [
        send(send_b, stat_b.at[index_b], r_send.at[d], r_recv.at[d], group_b[d]) for d in range(15)
    ]
    stat_b[index_b] = partial
    end_halo(halo_three, halves)
    for copy in stat_copies:
        copy.wait_recv()
    sums = stat_b[0]
    for i in range(1, 16):
        sums = sums + stat_b[i]
    intersection, denominator = sums[0:1], sums[1:2] + sums[2:3]
    loss_ref[...] = jnp.broadcast_to(1.0 - 2.0 * intersection / denominator, (8, 128))
    scale = LOSS_SCALE * 16384.0 * -2.0 / (denominator * denominator)
    for t in range(3):
        cells = halo_three[t, :, 256:384].astype(F32)
        factor = scale * (cells * denominator - intersection)
        factor = jnp.concatenate([factor, factor], axis=1)
        grad_two[t] = (halo_three[t, :, 0:256].astype(F32) * factor).astype(BF)
    grad_active = conv(grad_two, second, True)
    halo_four[1, 32:96] = (grad_active * slope_one).astype(BF)
    halves = start_halo(3, halo_four)
    end_halo(halo_four, halves)
    grad_neck = conv(halo_four, first, True).astype(BF)
    grad_ref[...] = lax.dot_general(grad_neck, neck[...], NT, preferred_element_type=F32).astype(BF)
    for copy in sent:
        copy.wait_send()


def decoder(attended, labels, w_full, residual, w_neck, w_first, w_second, w_class):
    dma = pltpu.SemaphoreType.DMA
    vmem, anywhere = pl.BlockSpec(memory_space=pltpu.VMEM), pl.BlockSpec(memory_space=pl.ANY)
    return pl.pallas_call(
        decoder_kernel,
        out_shape=(
            jax.ShapeDtypeStruct((64, 1024), BF),
            jax.ShapeDtypeStruct((8, 128), F32),
            jax.ShapeDtypeStruct((64, 1024), BF),
        ),
        in_specs=[vmem, vmem, anywhere, vmem, anywhere, anywhere, anywhere, vmem],
        out_specs=(vmem, vmem, vmem),
        scratch_shapes=[
            pltpu.VMEM((64, 1024), BF),
            pltpu.VMEM((1024, 1024), BF),
            pltpu.VMEM((1024, 256), BF),
            pltpu.VMEM((27, 256, 256), BF),
            pltpu.VMEM((27, 256, 256), BF),
            pltpu.VMEM((3, 128, 256), BF),
            pltpu.VMEM((3, 128, 256), BF),
            pltpu.VMEM((3, 128, 384), BF),
            pltpu.VMEM((3, 128, 256), BF),
            pltpu.VMEM((3, 128, 256), BF),
            pltpu.VMEM((16, 8, 128), F32),
            pltpu.VMEM((16, 8, 128), F32),
            pltpu.VMEM((8, 128), F32),
            pltpu.VMEM((8, 128), F32),
            dma((5,)),
            dma((7,)),
            dma((7,)),
            dma((4, 8)),
            dma((4, 8)),
            dma((15,)),
            dma((15,)),
            dma((15,)),
            dma((15,)),
        ],
        compiler_params=pltpu.CompilerParams(
            collective_id=1, has_side_effects=True, vmem_limit_bytes=40 << 20
        ),
        name="decoder",
    )(attended, labels, w_full, residual, w_neck, w_first, w_second, w_class)


def on_device(
    queries, key_rows, value_rows, residual, w_out, w_neck, w_first, w_second, w_class, labels
):
    label_rows = jnp.pad(labels.reshape(2, 32).astype(BF), ((0, 14), (0, 224)))
    attended, own_labels, w_full = attention(
        queries.reshape(TOK, 128), key_rows.reshape(TOK, 128), value_rows.reshape(TOK, 128), label_rows, w_out
    )
    encoded, loss, grad = decoder(
        attended,
        own_labels,
        w_full,
        residual.reshape(64, 1024),
        w_neck,
        w_first.reshape(27, 256, 256),
        w_second.reshape(27, 256, 256),
        jnp.broadcast_to(w_class[None, :], (16, 256)),
    )
    shape = residual.shape
    return (encoded.reshape(shape), loss[0, 0], grad.reshape(shape))


def solution(mesh):
    slab = P("tok", None, None, "heads")
    rows = P("heads", "tok", None, None)
    placed = (slab, slab, slab, rows, P("heads", None), P(), P(), P(), P(), P("heads", None, "tok"))
    return jax.shard_map(
        on_device, mesh=mesh, in_specs=placed, out_specs=(rows, P(), rows), check_vma=False
    )
```

```python
import jax
import jax.numpy as jnp
from jax import lax
from jax.experimental import pallas as pl
from jax.experimental.pallas import tpu as pltpu
from jax.sharding import PartitionSpec as P

MESH = pl.DeviceIdType.MESH
BF = jnp.bfloat16
F32 = jnp.float32
HD = 64
LOSS_SCALE = 64.0
LOG2E = 1.4426950408889634
NN = (((1,), (0,)), ((), ()))
NT = (((1,), (1,)), ((), ()))
TOK = 512
ROWS = 528
NZ = 8
SLOT = {(0, 0): 0, (0, 1): 1}
for _k in (1, 2, 3):
    _b = 4 * _k - 2
    SLOT.update({(-_k, 0): _b, (_k, 0): _b + 1, (-_k, 1): _b + 2, (_k, 1): _b + 3})
SLOT.update({(4, 0): 14, (4, 1): 15})
DISTANCE = [None] * 16
for _key, _slot in SLOT.items():
    DISTANCE[_slot] = _key
TILES = [(0, 1), (2, 3, 4, 5), (6, 7, 8, 9), (10, 11, 12, 13), (14, 15)]


def place():
    heads, tok = lax.axis_index("heads"), lax.axis_index("tok")
    return heads, tok, tok // 4, (tok // 2) % 2, tok % 2


def at(heads, tok):
    return {"heads": heads, "tok": tok}


NEAR = [(dh, dt) for dh in (-1, 0, 1) for dt in (-1, 0, 1) if (dh, dt) != (0, 0)]
PARTS = ((0, TOK // 2), (TOK // 2, ROWS))


def block_kernel(
    q_hbm, k_hbm, v_hbm, lab_ref, w_hbm, res_hbm, neck_hbm, first_hbm, second_hbm, class_hbm,
    enc_hbm, loss_ref, grad_hbm,
    kv, q_buf, qx, acc, peak, o_send, o_recv, lse_send, lse_recv, lab_send, lab_recv, attended,
    att_all, wf, neck, first, second, residual, w_class_buf, result,
    halo_one, halo_two, halo_three, halo_four, grad_two, stat_a, stat_b, send_a, send_b,
    local_sem, kv_send, kv_recv, mate_send, y_send, y_recv, w_send, w_recv,
    a_send, a_recv, h_send, h_recv, s_send, s_recv, r_send, r_recv,
):
    heads, tok, z, y, core = place()
    up = at(heads, (tok + 4) % (4 * NZ))
    down = at(heads, (tok + 4 * NZ - 4) % (4 * NZ))
    mate = at(heads, tok + 1 - 2 * core)
    across = at(heads, tok + 2 - 4 * y)
    others = [at((heads + d) % 8, tok) for d in range(1, 8)]
    near = [at((heads + dh + 8) % 8, (tok + dt + 32) % 32) for dh, dt in NEAR]
    group_a = [
        at((heads + d // 2) % 8, tok if d % 2 == 0 else tok + 1 - 2 * core) for d in range(1, 16)
    ]
    group_b = [
        at(heads, (tok + 4 * (d // 2)) % 32 if d % 2 == 0 else (tok + 4 * (d // 2) + 2 - 4 * y + 32) % 32)
        for d in range(1, 16)
    ]
    mine = pl.ds(pl.multiple_of(heads * 128, 128), 128)
    own_rows = pl.ds(pl.multiple_of(heads * 64, 64), 64)

    local = [
        pltpu.make_async_copy(k_hbm, kv.at[0, 0:TOK, 0:128], local_sem.at[0]),
        pltpu.make_async_copy(v_hbm, kv.at[0, 0:TOK, 128:256], local_sem.at[1]),
        pltpu.make_async_copy(q_hbm, q_buf.at[0], local_sem.at[2]),
        pltpu.make_async_copy(w_hbm, wf.at[mine], local_sem.at[3]),
    ]
    loads = [
        pltpu.make_async_copy(src, dst, local_sem.at[4 + i])
        for i, (src, dst) in enumerate(
            (
                (neck_hbm, neck),
                (first_hbm, first),
                (second_hbm, second),
                (res_hbm, residual),
                (class_hbm, w_class_buf),
            )
        )
    ]
    for copy in local:
        copy.start()
    barrier = pltpu.get_barrier_semaphore()
    peers = [up, down, mate, across] + others
    for peer in peers:
        pl.semaphore_signal(barrier, inc=1, device_id=peer, device_id_type=MESH)
    lab_rows = jnp.concatenate(
        [lab_ref[...].astype(F32), jnp.zeros((2, 224), F32)], axis=1
    )
    lab_rows = jnp.concatenate([lab_rows, jnp.zeros((14, 256), F32)], axis=0)
    kv[0, TOK:ROWS, :] = lab_rows.astype(BF)
    pl.semaphore_wait(barrier, len(peers))
    for copy in local:
        copy.wait()

    sent = []

    def send(src, dst, send_sem, recv_sem, peer):
        copy = pltpu.make_async_remote_copy(
            src_ref=src, dst_ref=dst, send_sem=send_sem, recv_sem=recv_sem, device_id=peer, device_id_type=MESH
        )
        copy.start()
        sent.append(copy)
        return copy

    arrivals = {}
    n_ring = [0]

    def ring(distance, part):
        slot = SLOT[(distance, 0)]
        lo, hi = PARTS[part]
        for step, peer in ((-1, up), (1, down)):
            if distance * step < 0:
                continue
            to = distance + step
            if abs(to) > 3:
                if part != (0 if step < 0 else 1):
                    continue
                to = 4
            dst = SLOT[(to, 0)]
            copy = send(
                kv.at[slot, lo:hi], kv.at[dst, lo:hi], kv_send.at[n_ring[0]], kv_recv.at[2 * dst + part], peer
            )
            n_ring[0] += 1
            arrivals[(to, 0, part)] = copy

    def share(distance, part):
        slot, dst = SLOT[(distance, 0)], SLOT[(distance, 1)]
        lo, hi = PARTS[part]
        arrivals[(distance, 1, part)] = send(
            kv.at[slot, lo:hi],
            kv.at[dst, lo:hi],
            mate_send.at[2 * slot + part],
            kv_recv.at[2 * dst + part],
            mate,
        )

    def arrive(k, part):
        for distance in (-k, k):
            arrivals[(distance, 0, part)].wait_recv()
            ring(distance, part)
            share(distance, part)

    def await_mate(*distances):
        for distance in distances:
            for part in range(2):
                arrivals[(distance, 1, part)].wait_recv()

    def prepare(half):
        lane = lax.broadcasted_iota(jnp.int32, (TOK, 128), 1)
        q = q_buf[half].astype(F32) * (HD**-0.5 * LOG2E)
        high = q.astype(BF)
        low = (q - high.astype(F32)).astype(BF)
        zero = jnp.zeros_like(high)
        rows = slice(half * TOK, (half + 1) * TOK)
        for h in range(2):
            mine_h = (lane < HD) if h == 0 else (lane >= HD)
            qx[h, rows, 0:128] = jnp.where(mine_h, high, zero)
            qx[h, rows, 128:256] = jnp.where(mine_h, low, zero)
        acc[rows] = jnp.zeros((TOK, 256), F32)
        peak[:, rows] = jnp.full((2, TOK, 128), -1e30, F32)

    def attend(half, slots):
        rows = slice(half * TOK, (half + 1) * TOK)
        lane = lax.broadcasted_iota(jnp.int32, (TOK, 128), 1)
        k = jnp.concatenate([kv[s, 0:TOK, 0:128] for s in slots], axis=0)
        kk = jnp.concatenate([k, k], axis=1)
        v = jnp.concatenate([kv[s, 0:TOK, 128:256] for s in slots], axis=0)
        vx = jnp.concatenate([v, jnp.ones_like(v)], axis=1)
        scores = [lax.dot_general(qx[h, rows, :], kk, NT, preferred_element_type=F32) for h in range(2)]
        sums, factors = [], []
        for h in range(2):
            old = peak[h, rows, :]
            new = jnp.maximum(old, jnp.max(scores[h], axis=1, keepdims=True))
            peak[h, rows, :] = new
            factors.append(jnp.exp2(old - new))
            mixing = jnp.exp2(scores[h] - new[:, :1]).astype(BF)
            sums.append(lax.dot_general(mixing, vx, NN, preferred_element_type=F32))
        factor = jnp.where(lane < HD, factors[0], factors[1])
        for part in (slice(0, 128), slice(128, 256)):
            acc[rows, part] = acc[rows, part] * factor + jnp.where(lane < HD, sums[0][:, part], sums[1][:, part])

    def finish(half):
        lane = lax.broadcasted_iota(jnp.int32, (TOK, 128), 1)
        rows = slice(half * TOK, (half + 1) * TOK)
        total = acc[rows, 128:256]
        top = jnp.where(lane < HD, peak[0, rows], peak[1, rows])
        return acc[rows, 0:128] / total, top + jnp.log(total) * LOG2E

    q_copy = send(q_buf.at[0], q_buf.at[1], y_send.at[0], y_recv.at[0], across)
    for part in range(2):
        ring(0, part)
    for part in range(2):
        share(0, part)
    prepare(0)
    await_mate(0)
    attend(0, TILES[0])
    w_copies = [send(wf.at[mine], wf.at[mine], w_send.at[d], w_recv.at[d], others[d]) for d in range(7)]
    for load in loads:
        load.start()
    q_copy.wait_recv()
    prepare(1)
    arrive(1, 0)
    attend(1, TILES[0])
    arrive(1, 1)
    await_mate(-1, 1)
    attend(0, TILES[1])
    arrive(2, 0)
    attend(1, TILES[1])
    arrive(2, 1)
    await_mate(-2, 2)
    attend(0, TILES[2])
    arrive(3, 0)
    attend(1, TILES[2])
    arrive(3, 1)
    await_mate(-3, 3)
    attend(1, TILES[3])
    for part in range(2):
        arrivals[(4, 0, part)].wait_recv()
        share(4, part)
    await_mate(4)
    attend(1, TILES[4])

    part, lse = finish(1)
    o_send[...] = part.astype(BF)
    flat = lse.T
    lse_send[0:8] = flat[0:8]
    lse_send[8:16] = flat[64:72]
    label_rows = jnp.concatenate([kv[s, TOK:ROWS, :] for s in range(16)], axis=0)
    row = lax.broadcasted_iota(jnp.int32, (64, 256), 0)
    col = lax.broadcasted_iota(jnp.int32, (64, 256), 1)
    pick = jnp.zeros((64, 256), jnp.bool_)
    for s, (distance, other) in enumerate(DISTANCE):
        owner_core = core if other == 0 else 1 - core
        owner = ((z + distance + NZ) % NZ) * 4 + y * 2 + owner_core
        pick = pick | (((row % 32) == owner) & (col == 16 * s + row // 32))
    by_depth = lax.dot_general(
        jnp.where(pick, 1.0, 0.0).astype(BF), label_rows, NN, preferred_element_type=F32
    )

    def at_depth(depth):
        chosen = jnp.sum(jnp.where(col == depth, by_depth, 0.0), axis=1, keepdims=True)
        return jnp.broadcast_to(chosen, (64, 128))

    lab_send[...] = at_depth(tok + 2 - 4 * y)
    o_copy = send(o_send, o_recv, y_send.at[1], y_recv.at[1], across)
    lse_copy = send(lse_send, lse_recv, y_send.at[2], y_recv.at[2], across)
    lab_copy = send(lab_send, lab_recv, y_send.at[3], y_recv.at[3], across)
    attend(0, TILES[3])
    attend(0, TILES[4])
    own_part, my_lse = finish(0)
    lse_copy.wait_recv()
    head0 = jnp.broadcast_to(lse_recv[0:1], (64, TOK))
    head1 = jnp.broadcast_to(lse_recv[8:9], (64, TOK))
    its_lse = jnp.concatenate([head0, head1], axis=0).T
    top = jnp.maximum(my_lse, its_lse)
    my_share, its_share = jnp.exp2(my_lse - top), jnp.exp2(its_lse - top)
    both = my_share + its_share
    o_copy.wait_recv()
    merged = (my_share * own_part + its_share * o_recv[...].astype(F32)) / both
    attended[...] = merged.astype(BF)

    own = pltpu.make_async_copy(attended.at[own_rows], att_all.at[:, mine], local_sem.at[9])
    own.start()
    copies = []
    for i in range(7):
        theirs = lax.rem(heads + i + 1, 8)
        copies.append(
            send(
                attended.at[pl.ds(pl.multiple_of(theirs * 64, 64), 64)],
                att_all.at[:, mine],
                a_send.at[i],
                a_recv.at[i],
                others[i],
            )
        )
    lab_copy.wait_recv()
    labels = at_depth(tok) + lab_recv[...]

    def start_halo(stage, halo):
        halves = []
        for i, (dh, dt) in enumerate(NEAR):
            src, dst = {0: ((32, 96), (32, 96)), 1: ((64, 96), (0, 32)), -1: ((32, 64), (96, 128))}[dh]
            halves.append(
                send(
                    halo.at[1, src[0] : src[1]],
                    halo.at[1 - dt, dst[0] : dst[1]],
                    h_send.at[stage, i],
                    h_recv.at[stage, i],
                    near[i],
                )
            )
        return halves

    def end_halo(halo, halves):
        width = halo.shape[2]
        for copy in halves:
            copy.wait_recv()

        @pl.when(heads == 0)
        def _():
            halo[:, 0:32] = jnp.zeros((3, 32, width), BF)

        @pl.when(heads == 7)
        def _():
            halo[:, 96:128] = jnp.zeros((3, 32, width), BF)

        @pl.when(tok == 0)
        def _():
            halo[0] = jnp.zeros((128, width), BF)

        @pl.when(tok == 31)
        def _():
            halo[2] = jnp.zeros((128, width), BF)

    def conv(halo, weights, flipped):
        groups = halo.shape[2] // 256
        parts = []
        for e in range(3):
            total = None
            for a in range(3):
                for b in range(3):
                    c, t = (2 - a, 2 - b) if flipped else (a, b)
                    window = [halo[t, 32 * c : 32 * c + 64, 256 * g : 256 * g + 256] for g in range(groups)]
                    term = lax.dot_general(
                        jnp.concatenate(window, axis=0),
                        weights[(a * 3 + b) * 3 + e],
                        NT if flipped else NN,
                        preferred_element_type=F32,
                    )
                    total = term if total is None else total + term
            parts.append(total)
        if flipped:
            parts = parts[::-1]
        rows = 64 * groups
        inline = lax.broadcasted_iota(jnp.int32, (rows, 256), 0) % 32
        before = jnp.where(inline == 0, 0.0, pltpu.roll(parts[0], 1, 0))
        after = jnp.where(inline == 31, 0.0, pltpu.roll(parts[2], rows - 1, 0))
        return before + parts[1] + after

    def sigmoid(v):
        return 1.0 / (1.0 + jnp.exp(-v))

    for load in loads:
        load.wait()
    for copy in w_copies:
        copy.wait_recv()
    own.wait()
    for copy in copies:
        copy.wait_recv()
    projected = lax.dot_general(att_all[...], wf[...], NN, preferred_element_type=F32)
    encoded = (residual[...].astype(F32) + projected).astype(BF)
    halo_one[1, 32:96] = lax.dot_general(encoded, neck[...], NN, preferred_element_type=F32).astype(BF)
    halves = start_halo(0, halo_one)
    result[0] = encoded
    enc_copy = pltpu.make_async_copy(result.at[0], enc_hbm, local_sem.at[10])
    enc_copy.start()
    end_halo(halo_one, halves)
    hidden_one = conv(halo_one, first, False)
    gate_one = sigmoid(hidden_one)
    halo_two[1, 32:96] = (hidden_one * gate_one).astype(BF)
    halves = start_halo(1, halo_two)
    slope_one = gate_one * (1.0 + hidden_one * (1.0 - gate_one))
    end_halo(halo_two, halves)
    hidden_two = conv(halo_two, second, False)
    gate_two = sigmoid(hidden_two)
    active_two = (hidden_two * gate_two).astype(BF).astype(F32)
    w_class = w_class_buf[...].astype(F32)
    logits = jnp.sum(active_two * w_class, axis=1, keepdims=True)
    probability = jnp.broadcast_to(sigmoid(logits), (64, 128))
    spread = probability * (1.0 - probability)
    slope_two = gate_two * (1.0 + hidden_two * (1.0 - gate_two))
    unscaled = jnp.concatenate([spread, spread], axis=1) * w_class * slope_two
    halo_three[1, 32:96, 0:256] = unscaled.astype(BF)
    halo_three[1, 32:96, 256:384] = labels.astype(BF)
    halves = start_halo(2, halo_three)

    def over_cells(value):
        return jnp.sum(value, axis=0, keepdims=True)

    row8 = lax.broadcasted_iota(jnp.int32, (8, 128), 0)
    stats = jnp.where(
        row8 == 0,
        over_cells(probability * labels),
        jnp.where(row8 == 1, over_cells(probability), over_cells(labels)),
    )
    index_a = heads * 2 + core
    send_a[...] = stats
    stat_copies = [
        send(send_a, stat_a.at[index_a], s_send.at[d], s_recv.at[d], group_a[d]) for d in range(15)
    ]
    stat_a[index_a] = stats
    end_halo(halo_three, halves)
    for copy in stat_copies:
        copy.wait_recv()
    partial = stat_a[0]
    for i in range(1, 16):
        partial = partial + stat_a[i]
    index_b = z * 2 + y
    send_b[...] = partial
    stat_copies = [
        send(send_b, stat_b.at[index_b], r_send.at[d], r_recv.at[d], group_b[d]) for d in range(15)
    ]
    stat_b[index_b] = partial
    for t in range(3):
        cells = halo_three[t, :, 256:384]
        cells = jnp.concatenate([cells, cells], axis=1).astype(F32)
        slopes = halo_three[t, :, 0:256].astype(F32)
        grad_two[t, :, 0:256] = (slopes * cells).astype(BF)
        grad_two[t, :, 256:512] = (slopes * (1.0 - cells)).astype(BF)
    grad_active = conv(grad_two, second, True)
    halo_four[1, 32:96, 0:256] = (grad_active[0:64] * slope_one).astype(BF)
    halo_four[1, 32:96, 256:512] = (grad_active[64:128] * slope_one).astype(BF)
    halves = start_halo(3, halo_four)
    end_halo(halo_four, halves)
    by_kind = conv(halo_four, first, True)
    for copy in stat_copies:
        copy.wait_recv()
    sums = stat_b[0]
    for i in range(1, 16):
        sums = sums + stat_b[i]
    intersection, denominator = sums[0:1], sums[1:2] + sums[2:3]
    loss_ref[0, 0] = (1.0 - 2.0 * intersection / denominator)[0, 0]
    scale = LOSS_SCALE * 16384.0 * -2.0 / (denominator * denominator)
    fault, rest = scale * (denominator - intersection), scale * -intersection
    fault, rest = jnp.concatenate([fault, fault], axis=1), jnp.concatenate([rest, rest], axis=1)
    grad_neck = (by_kind[0:64] * fault + by_kind[64:128] * rest).astype(BF)
    result[1] = lax.dot_general(grad_neck, neck[...], NT, preferred_element_type=F32).astype(BF)
    grad_copy = pltpu.make_async_copy(result.at[1], grad_hbm, local_sem.at[11])
    grad_copy.start()
    enc_copy.wait()
    for copy in sent:
        copy.wait_send()
    grad_copy.wait()


def block(queries, key_rows, value_rows, labels, w_out, residual, w_neck, w_first, w_second, w_class):
    dma = pltpu.SemaphoreType.DMA
    vmem, anywhere = pl.BlockSpec(memory_space=pltpu.VMEM), pl.BlockSpec(memory_space=pl.ANY)
    return pl.pallas_call(
        block_kernel,
        out_shape=(
            jax.ShapeDtypeStruct((64, 1024), BF),
            jax.ShapeDtypeStruct((1, 1), F32),
            jax.ShapeDtypeStruct((64, 1024), BF),
        ),
        in_specs=[anywhere] * 3 + [vmem] + [anywhere] * 6,
        out_specs=(anywhere, pl.BlockSpec(memory_space=pltpu.SMEM), anywhere),
        scratch_shapes=[
            pltpu.VMEM((16, ROWS, 256), BF),
            pltpu.VMEM((2, TOK, 128), BF),
            pltpu.VMEM((2, 2 * TOK, 256), BF),
            pltpu.VMEM((2 * TOK, 256), F32),
            pltpu.VMEM((2, 2 * TOK, 128), F32),
            pltpu.VMEM((TOK, 128), BF),
            pltpu.VMEM((TOK, 128), BF),
            pltpu.VMEM((16, TOK), F32),
            pltpu.VMEM((16, TOK), F32),
            pltpu.VMEM((64, 128), F32),
            pltpu.VMEM((64, 128), F32),
            pltpu.VMEM((TOK, 128), BF),
            pltpu.VMEM((64, 1024), BF),
            pltpu.VMEM((1024, 1024), BF),
            pltpu.VMEM((1024, 256), BF),
            pltpu.VMEM((27, 256, 256), BF),
            pltpu.VMEM((27, 256, 256), BF),
            pltpu.VMEM((64, 1024), BF),
            pltpu.VMEM((1, 256), BF),
            pltpu.VMEM((2, 64, 1024), BF),
            pltpu.VMEM((3, 128, 256), BF),
            pltpu.VMEM((3, 128, 256), BF),
            pltpu.VMEM((3, 128, 384), BF),
            pltpu.VMEM((3, 128, 512), BF),
            pltpu.VMEM((3, 128, 512), BF),
            pltpu.VMEM((16, 8, 128), F32),
            pltpu.VMEM((16, 8, 128), F32),
            pltpu.VMEM((8, 128), F32),
            pltpu.VMEM((8, 128), F32),
            dma((12,)),
            dma((16,)),
            dma((32,)),
            dma((32,)),
            dma((4,)),
            dma((4,)),
            dma((7,)),
            dma((7,)),
            dma((7,)),
            dma((7,)),
            dma((4, 8)),
            dma((4, 8)),
            dma((15,)),
            dma((15,)),
            dma((15,)),
            dma((15,)),
        ],
        compiler_params=pltpu.CompilerParams(
            collective_id=0, has_side_effects=True, vmem_limit_bytes=67043328
        ),
        name="block",
    )(queries, key_rows, value_rows, labels, w_out, residual, w_neck, w_first, w_second, w_class)


def on_device(
    queries, key_rows, value_rows, residual, w_out, w_neck, w_first, w_second, w_class, labels
):
    encoded, loss, grad = block(
        queries.reshape(TOK, 128),
        key_rows.reshape(TOK, 128),
        value_rows.reshape(TOK, 128),
        labels.reshape(2, 32),
        w_out,
        residual.reshape(64, 1024),
        w_neck,
        w_first.reshape(27, 256, 256),
        w_second.reshape(27, 256, 256),
        w_class.reshape(1, 256),
    )
    shape = residual.shape
    return (encoded.reshape(shape), loss.reshape(()), grad.reshape(shape))


def solution(mesh):
    slab = P("tok", None, None, "heads")
    rows = P("heads", "tok", None, None)
    placed = (slab, slab, slab, rows, P("heads", None), P(), P(), P(), P(), P("heads", None, "tok"))
    return jax.shard_map(
        on_device, mesh=mesh, in_specs=placed, out_specs=(rows, P(), rows), check_vma=False
    )
```

```python
import jax
import jax.numpy as jnp
from jax import lax
from jax.experimental import pallas as pl
from jax.experimental.pallas import tpu as pltpu
from jax.sharding import PartitionSpec as P

MESH = pl.DeviceIdType.MESH
BF = jnp.bfloat16
F32 = jnp.float32
HD = 64
LOSS_SCALE = 64.0
LOG2E = 1.4426950408889634
NN = (((1,), (0,)), ((), ()))
NT = (((1,), (1,)), ((), ()))
TOK = 512
ROWS = 528
NZ = 8
SLOT = {(0, 0): 0, (0, 1): 1}
for _k in (1, 2, 3):
    _b = 4 * _k - 2
    SLOT.update({(-_k, 0): _b, (_k, 0): _b + 1, (-_k, 1): _b + 2, (_k, 1): _b + 3})
SLOT.update({(4, 0): 14, (4, 1): 15})
DISTANCE = [None] * 16
for _key, _slot in SLOT.items():
    DISTANCE[_slot] = _key
TILES = [(0, 1), (2, 3, 4, 5), (6, 7, 8, 9), (10, 11, 12, 13), (14, 15)]


def place():
    heads, tok = lax.axis_index("heads"), lax.axis_index("tok")
    return heads, tok, tok // 4, (tok // 2) % 2, tok % 2


def at(heads, tok):
    return {"heads": heads, "tok": tok}


FAR, OWN, MATE = 0, 1, 2
NEAR = [(0, FAR), (1, FAR), (-1, FAR), (1, OWN), (-1, OWN), (1, MATE), (-1, MATE), (0, MATE)]
PARTS = ((0, TOK // 2), (TOK // 2, ROWS))


def block_kernel(
    q_hbm, k_hbm, v_hbm, lab_ref, w_hbm, res_hbm, neck_hbm, first_hbm, second_hbm, class_ref,
    enc_hbm, loss_ref, grad_hbm,
    kv, q_buf, qx, acc, peak, o_send, o_recv, lse_send, lse_recv, lab_send, lab_recv, attended,
    att_all, wf, neck, first, second, residual, result,
    halo_one, halo_two, halo_three, halo_four, grad_two, stat_a, stat_b, send_a, send_b,
    local_sem, kv_send, kv_recv, mate_send, y_send, y_recv, w_send, w_recv,
    a_send, a_recv, h_send, h_recv, s_send, s_recv, r_send, r_recv,
):
    heads, tok, z, y, core = place()
    up = at(heads, (tok + 4) % (4 * NZ))
    down = at(heads, (tok + 4 * NZ - 4) % (4 * NZ))
    mate = at(heads, tok + 1 - 2 * core)
    across = at(heads, tok + 2 - 4 * y)
    others = [at((heads + d) % 8, tok) for d in range(1, 8)]
    beside = {FAR: (tok + 31 + 2 * core) % 32, OWN: tok, MATE: tok + 1 - 2 * core}
    near = [at((heads + dh + 8) % 8, beside[plane]) for dh, plane in NEAR]
    group_a = [
        at((heads + d // 2) % 8, tok if d % 2 == 0 else tok + 1 - 2 * core) for d in range(1, 16)
    ]
    group_b = [
        at(heads, (tok + 4 * (d // 2)) % 32 if d % 2 == 0 else (tok + 4 * (d // 2) + 2 - 4 * y + 32) % 32)
        for d in range(1, 16)
    ]
    mine = pl.ds(pl.multiple_of(heads * 128, 128), 128)
    own_rows = pl.ds(pl.multiple_of(heads * 64, 64), 64)

    local = [
        pltpu.make_async_copy(k_hbm, kv.at[0, 0:TOK, 0:128], local_sem.at[0]),
        pltpu.make_async_copy(v_hbm, kv.at[0, 0:TOK, 128:256], local_sem.at[1]),
        pltpu.make_async_copy(q_hbm, q_buf.at[0], local_sem.at[2]),
        pltpu.make_async_copy(w_hbm, wf.at[mine], local_sem.at[3]),
    ]
    loads = [
        pltpu.make_async_copy(src, dst, local_sem.at[4 + i])
        for i, (src, dst) in enumerate(
            (
                (neck_hbm, neck),
                (first_hbm, first),
                (second_hbm, second),
                (res_hbm, residual),
            )
        )
    ]
    for copy in local:
        copy.start()
    barrier = pltpu.get_barrier_semaphore()
    peers = [up, down, mate, across] + others
    for peer in peers:
        pl.semaphore_signal(barrier, inc=1, device_id=peer, device_id_type=MESH)
    lab_rows = jnp.concatenate(
        [lab_ref[...].astype(F32), jnp.zeros((2, 224), F32)], axis=1
    )
    lab_rows = jnp.concatenate([lab_rows, jnp.zeros((14, 256), F32)], axis=0)
    kv[0, TOK:ROWS, :] = lab_rows.astype(BF)

    sent = []

    def send(src, dst, send_sem, recv_sem, peer):
        copy = pltpu.make_async_remote_copy(
            src_ref=src, dst_ref=dst, send_sem=send_sem, recv_sem=recv_sem, device_id=peer, device_id_type=MESH
        )
        copy.start()
        sent.append(copy)
        return copy

    arrivals = {}
    n_ring = [0]

    def ring(distance, part):
        slot = SLOT[(distance, 0)]
        lo, hi = PARTS[part]
        for step, peer in ((-1, up), (1, down)):
            if distance * step < 0:
                continue
            to = distance + step
            if abs(to) > 3:
                if part != (0 if step < 0 else 1):
                    continue
                to = 4
            dst = SLOT[(to, 0)]
            copy = send(
                kv.at[slot, lo:hi], kv.at[dst, lo:hi], kv_send.at[n_ring[0]], kv_recv.at[2 * dst + part], peer
            )
            n_ring[0] += 1
            arrivals[(to, 0, part)] = copy

    def share(distance, part):
        slot, dst = SLOT[(distance, 0)], SLOT[(distance, 1)]
        lo, hi = PARTS[part]
        arrivals[(distance, 1, part)] = send(
            kv.at[slot, lo:hi],
            kv.at[dst, lo:hi],
            mate_send.at[2 * slot + part],
            kv_recv.at[2 * dst + part],
            mate,
        )

    def arrive(k, part):
        for distance in (-k, k):
            arrivals[(distance, 0, part)].wait_recv()
            ring(distance, part)
            share(distance, part)

    def await_mate(*distances):
        for distance in distances:
            for part in range(2):
                arrivals[(distance, 1, part)].wait_recv()

    def prepare(half):
        lane = lax.broadcasted_iota(jnp.int32, (TOK, 128), 1)
        q = q_buf[half].astype(F32) * (HD**-0.5 * LOG2E)
        high = q.astype(BF)
        low = (q - high.astype(F32)).astype(BF)
        zero = jnp.zeros_like(high)
        rows = slice(half * TOK, (half + 1) * TOK)
        for h in range(2):
            mine_h = (lane < HD) if h == 0 else (lane >= HD)
            qx[h, rows, 0:128] = jnp.where(mine_h, high, zero)
            qx[h, rows, 128:256] = jnp.where(mine_h, low, zero)
        acc[rows] = jnp.zeros((TOK, 256), F32)
        peak[:, rows] = jnp.full((2, TOK, 128), -1e30, F32)

    def attend(half, slots):
        rows = slice(half * TOK, (half + 1) * TOK)
        lane = lax.broadcasted_iota(jnp.int32, (TOK, 128), 1)
        k = jnp.concatenate([kv[s, 0:TOK, 0:128] for s in slots], axis=0)
        kk = jnp.concatenate([k, k], axis=1)
        v = jnp.concatenate([kv[s, 0:TOK, 128:256] for s in slots], axis=0)
        vx = jnp.concatenate([v, jnp.ones_like(v)], axis=1)
        scores = [lax.dot_general(qx[h, rows, :], kk, NT, preferred_element_type=F32) for h in range(2)]
        sums, factors = [], []
        for h in range(2):
            old = peak[h, rows, :]
            new = jnp.maximum(old, jnp.max(scores[h], axis=1, keepdims=True))
            peak[h, rows, :] = new
            factors.append(jnp.exp2(old - new))
            mixing = jnp.exp2(scores[h] - new[:, :1]).astype(BF)
            sums.append(lax.dot_general(mixing, vx, NN, preferred_element_type=F32))
        factor = jnp.where(lane < HD, factors[0], factors[1])
        for part in (slice(0, 128), slice(128, 256)):
            acc[rows, part] = acc[rows, part] * factor + jnp.where(lane < HD, sums[0][:, part], sums[1][:, part])

    def finish(half):
        lane = lax.broadcasted_iota(jnp.int32, (TOK, 128), 1)
        rows = slice(half * TOK, (half + 1) * TOK)
        total = acc[rows, 128:256]
        top = jnp.where(lane < HD, peak[0, rows], peak[1, rows])
        return acc[rows, 0:128] / total, top + jnp.log(total) * LOG2E

    for copy in local:
        copy.wait()
    prepare(0)
    pl.semaphore_wait(barrier, len(peers))
    q_copy = send(q_buf.at[0], q_buf.at[1], y_send.at[0], y_recv.at[0], across)
    for part in range(2):
        ring(0, part)
    for part in range(2):
        share(0, part)
    w_copies = [send(wf.at[mine], wf.at[mine], w_send.at[d], w_recv.at[d], others[d]) for d in (3, 2, 4, 1, 5, 0, 6)]
    await_mate(0)
    attend(0, TILES[0])
    for load in loads:
        load.start()
    q_copy.wait_recv()
    prepare(1)
    arrive(1, 0)
    attend(1, TILES[0])
    arrive(1, 1)
    await_mate(-1, 1)
    attend(0, TILES[1])
    arrive(2, 0)
    attend(1, TILES[1])
    arrive(2, 1)
    await_mate(-2, 2)
    attend(0, TILES[2])
    arrive(3, 0)
    attend(1, TILES[2])
    arrive(3, 1)
    await_mate(-3, 3)
    attend(1, TILES[3])
    for part in range(2):
        arrivals[(4, 0, part)].wait_recv()
        share(4, part)
    await_mate(4)
    attend(1, TILES[4])

    part, lse = finish(1)
    o_send[...] = part.astype(BF)
    flat = lse.T
    row8 = lax.broadcasted_iota(jnp.int32, (8, TOK), 0)
    lse_send[...] = jnp.where(row8 < 4, jnp.broadcast_to(flat[0:1], (8, TOK)), jnp.broadcast_to(flat[64:65], (8, TOK)))
    label_rows = jnp.concatenate([kv[s, TOK:ROWS, :] for s in range(16)], axis=0)
    row = lax.broadcasted_iota(jnp.int32, (64, 256), 0)
    col = lax.broadcasted_iota(jnp.int32, (64, 256), 1)
    pick = jnp.zeros((64, 256), jnp.bool_)
    for s, (distance, other) in enumerate(DISTANCE):
        owner_core = core if other == 0 else 1 - core
        owner = ((z + distance + NZ) % NZ) * 4 + y * 2 + owner_core
        pick = pick | (((row % 32) == owner) & (col == 16 * s + row // 32))
    by_depth = lax.dot_general(
        jnp.where(pick, 1.0, 0.0).astype(BF), label_rows, NN, preferred_element_type=F32
    )

    def at_depth(depth):
        chosen = jnp.sum(jnp.where(col == depth, by_depth, 0.0), axis=1, keepdims=True)
        return jnp.broadcast_to(chosen, (64, 128))

    lab_send[...] = at_depth(tok + 2 - 4 * y).astype(BF)
    o_copy = send(o_send, o_recv, y_send.at[1], y_recv.at[1], across)
    lse_copy = send(lse_send, lse_recv, y_send.at[2], y_recv.at[2], across)
    lab_copy = send(lab_send, lab_recv, y_send.at[3], y_recv.at[3], across)
    attend(0, TILES[3])
    attend(0, TILES[4])
    own_part, my_lse = finish(0)
    lse_copy.wait_recv()
    head0 = jnp.broadcast_to(lse_recv[0:1], (64, TOK))
    head1 = jnp.broadcast_to(lse_recv[4:5], (64, TOK))
    its_lse = jnp.concatenate([head0, head1], axis=0).T
    top = jnp.maximum(my_lse, its_lse)
    my_share, its_share = jnp.exp2(my_lse - top), jnp.exp2(its_lse - top)
    both = my_share + its_share
    o_copy.wait_recv()
    merged = (my_share * own_part + its_share * o_recv[...].astype(F32)) / both
    attended[...] = merged.astype(BF)

    own = pltpu.make_async_copy(attended.at[own_rows], att_all.at[:, mine], local_sem.at[9])
    own.start()
    copies = []
    for i in range(7):
        theirs = lax.rem(heads + i + 1, 8)
        copies.append(
            send(
                attended.at[pl.ds(pl.multiple_of(theirs * 64, 64), 64)],
                att_all.at[:, mine],
                a_send.at[i],
                a_recv.at[i],
                others[i],
            )
        )
    lab_copy.wait_recv()
    labels = at_depth(tok) + lab_recv[...].astype(F32)

    def start_halo(stage, halo):
        halves = []
        for i, (dh, plane) in enumerate(NEAR):
            src, dst = {0: ((32, 96), (32, 96)), 1: ((64, 96), (0, 32)), -1: ((32, 64), (96, 128))}[dh]
            halves.append(
                send(
                    halo.at[OWN, src[0] : src[1]],
                    halo.at[plane, dst[0] : dst[1]],
                    h_send.at[stage, i],
                    h_recv.at[stage, i],
                    near[i],
                )
            )
        return halves

    def end_plane(halo, halves, plane):
        width = halo.shape[2]
        for copy, (_, its_plane) in zip(halves, NEAR):
            if its_plane == plane:
                copy.wait_recv()

        @pl.when(heads == 0)
        def _():
            halo[plane, 0:32] = jnp.zeros((32, width), BF)

        @pl.when(heads == 7)
        def _():
            halo[plane, 96:128] = jnp.zeros((32, width), BF)

        if plane == FAR:

            @pl.when((tok == 0) | (tok == 31))
            def _():
                halo[plane] = jnp.zeros((128, width), BF)

    def conv(halo, ready, weights, flipped):
        groups = halo.shape[2] // 256
        parts = [None] * 3
        for plane in (OWN, MATE, FAR):
            ready(plane)
            away = {OWN: 1, MATE: 2 - 2 * core, FAR: 2 * core}[plane]
            b = 2 - away if flipped else away
            for a in range(3):
                c = 2 - a if flipped else a
                window = [halo[plane, 32 * c : 32 * c + 64, 256 * g : 256 * g + 256] for g in range(groups)]
                window = jnp.concatenate(window, axis=0)
                for e in range(3):
                    term = lax.dot_general(
                        window, weights[(a * 3 + b) * 3 + e], NT if flipped else NN, preferred_element_type=F32
                    )
                    parts[e] = term if parts[e] is None else parts[e] + term
        if flipped:
            parts = parts[::-1]
        rows = 64 * groups
        inline = lax.broadcasted_iota(jnp.int32, (rows, 256), 0) % 32
        before = jnp.where(inline == 0, 0.0, pltpu.roll(parts[0], 1, 0))
        after = jnp.where(inline == 31, 0.0, pltpu.roll(parts[2], rows - 1, 0))
        return before + parts[1] + after

    def sigmoid(v):
        return 1.0 / (1.0 + jnp.exp(-v))

    for load in loads:
        load.wait()
    for copy in w_copies:
        copy.wait_recv()
    own.wait()
    for copy in copies:
        copy.wait_recv()
    projected = lax.dot_general(att_all[...], wf[...], NN, preferred_element_type=F32)
    encoded = (residual[...].astype(F32) + projected).astype(BF)
    halo_one[1, 32:96] = lax.dot_general(encoded, neck[...], NN, preferred_element_type=F32).astype(BF)
    halves_one = start_halo(0, halo_one)
    result[0] = encoded
    enc_copy = pltpu.make_async_copy(result.at[0], enc_hbm, local_sem.at[10])
    enc_copy.start()
    hidden_one = conv(halo_one, lambda plane: end_plane(halo_one, halves_one, plane), first, False)
    gate_one = sigmoid(hidden_one)
    halo_two[1, 32:96] = (hidden_one * gate_one).astype(BF)
    halves_two = start_halo(1, halo_two)
    slope_one = gate_one * (1.0 + hidden_one * (1.0 - gate_one))
    hidden_two = conv(halo_two, lambda plane: end_plane(halo_two, halves_two, plane), second, False)
    gate_two = sigmoid(hidden_two)
    active_two = (hidden_two * gate_two).astype(BF).astype(F32)
    w_class = class_ref[...].reshape(1, 256).astype(F32)
    logits = jnp.sum(active_two * w_class, axis=1, keepdims=True)
    probability = jnp.broadcast_to(sigmoid(logits), (64, 128))
    spread = probability * (1.0 - probability)
    slope_two = gate_two * (1.0 + hidden_two * (1.0 - gate_two))
    unscaled = jnp.concatenate([spread, spread], axis=1) * w_class * slope_two
    halo_three[1, 32:96, 0:256] = unscaled.astype(BF)
    halo_three[1, 32:96, 256:384] = labels.astype(BF)
    halves_three = start_halo(2, halo_three)

    def over_cells(value):
        return jnp.sum(value, axis=0, keepdims=True)

    row8 = lax.broadcasted_iota(jnp.int32, (8, 128), 0)
    stats = jnp.where(
        row8 == 0,
        over_cells(probability * labels),
        jnp.where(row8 == 1, over_cells(probability), over_cells(labels)),
    )
    index_a = heads * 2 + core
    send_a[...] = stats
    stat_copies = [
        send(send_a, stat_a.at[index_a], s_send.at[d], s_recv.at[d], group_a[d]) for d in range(15)
    ]
    stat_a[index_a] = stats
    index_b = z * 2 + y

    def split_kinds(plane):
        end_plane(halo_three, halves_three, plane)
        cells = halo_three[plane, :, 256:384]
        cells = jnp.concatenate([cells, cells], axis=1).astype(F32)
        slopes = halo_three[plane, :, 0:256].astype(F32)
        grad_two[plane, :, 0:256] = (slopes * cells).astype(BF)
        grad_two[plane, :, 256:512] = (slopes * (1.0 - cells)).astype(BF)

    grad_active = conv(grad_two, split_kinds, second, True)
    halo_four[1, 32:96, 0:256] = (grad_active[0:64] * slope_one).astype(BF)
    halo_four[1, 32:96, 256:512] = (grad_active[64:128] * slope_one).astype(BF)
    halves_four = start_halo(3, halo_four)
    for copy in stat_copies:
        copy.wait_recv()
    partial = stat_a[0]
    for i in range(1, 16):
        partial = partial + stat_a[i]
    send_b[...] = partial
    total_copies = [
        send(send_b, stat_b.at[index_b], r_send.at[d], r_recv.at[d], group_b[d]) for d in range(15)
    ]
    stat_b[index_b] = partial
    by_kind = conv(halo_four, lambda plane: end_plane(halo_four, halves_four, plane), first, True)
    for copy in total_copies:
        copy.wait_recv()
    sums = stat_b[0]
    for i in range(1, 16):
        sums = sums + stat_b[i]
    intersection, denominator = sums[0:1], sums[1:2] + sums[2:3]
    loss_ref[0, 0] = (1.0 - 2.0 * intersection / denominator)[0, 0]
    scale = LOSS_SCALE * 16384.0 * -2.0 / (denominator * denominator)
    fault, rest = scale * (denominator - intersection), scale * -intersection
    fault, rest = jnp.concatenate([fault, fault], axis=1), jnp.concatenate([rest, rest], axis=1)
    grad_neck = (by_kind[0:64] * fault + by_kind[64:128] * rest).astype(BF)
    result[1] = lax.dot_general(grad_neck, neck[...], NT, preferred_element_type=F32).astype(BF)
    grad_copy = pltpu.make_async_copy(result.at[1], grad_hbm, local_sem.at[11])
    grad_copy.start()
    enc_copy.wait()
    for copy in sent:
        copy.wait_send()
    grad_copy.wait()


def block(queries, key_rows, value_rows, labels, w_out, residual, w_neck, w_first, w_second, w_class):
    dma = pltpu.SemaphoreType.DMA
    vmem, anywhere = pl.BlockSpec(memory_space=pltpu.VMEM), pl.BlockSpec(memory_space=pl.ANY)
    return pl.pallas_call(
        block_kernel,
        out_shape=(
            jax.ShapeDtypeStruct((64, 1024), BF),
            jax.ShapeDtypeStruct((1, 1), F32),
            jax.ShapeDtypeStruct((64, 1024), BF),
        ),
        in_specs=[anywhere] * 3 + [vmem] + [anywhere] * 5 + [vmem],
        out_specs=(anywhere, pl.BlockSpec(memory_space=pltpu.SMEM), anywhere),
        scratch_shapes=[
            pltpu.VMEM((16, ROWS, 256), BF),
            pltpu.VMEM((2, TOK, 128), BF),
            pltpu.VMEM((2, 2 * TOK, 256), BF),
            pltpu.VMEM((2 * TOK, 256), F32),
            pltpu.VMEM((2, 2 * TOK, 128), F32),
            pltpu.VMEM((TOK, 128), BF),
            pltpu.VMEM((TOK, 128), BF),
            pltpu.VMEM((8, TOK), F32),
            pltpu.VMEM((8, TOK), F32),
            pltpu.VMEM((64, 128), BF),
            pltpu.VMEM((64, 128), BF),
            pltpu.VMEM((TOK, 128), BF),
            pltpu.VMEM((64, 1024), BF),
            pltpu.VMEM((1024, 1024), BF),
            pltpu.VMEM((1024, 256), BF),
            pltpu.VMEM((27, 256, 256), BF),
            pltpu.VMEM((27, 256, 256), BF),
            pltpu.VMEM((64, 1024), BF),
            pltpu.VMEM((2, 64, 1024), BF),
            pltpu.VMEM((3, 128, 256), BF),
            pltpu.VMEM((3, 128, 256), BF),
            pltpu.VMEM((3, 128, 384), BF),
            pltpu.VMEM((3, 128, 512), BF),
            pltpu.VMEM((3, 128, 512), BF),
            pltpu.VMEM((16, 8, 128), F32),
            pltpu.VMEM((16, 8, 128), F32),
            pltpu.VMEM((8, 128), F32),
            pltpu.VMEM((8, 128), F32),
            dma((12,)),
            dma((16,)),
            dma((32,)),
            dma((32,)),
            dma((4,)),
            dma((4,)),
            dma((7,)),
            dma((7,)),
            dma((7,)),
            dma((7,)),
            dma((4, 8)),
            dma((4, 8)),
            dma((15,)),
            dma((15,)),
            dma((15,)),
            dma((15,)),
        ],
        compiler_params=pltpu.CompilerParams(
            collective_id=0, has_side_effects=True, vmem_limit_bytes=67043328
        ),
        name="block",
    )(queries, key_rows, value_rows, labels, w_out, residual, w_neck, w_first, w_second, w_class)


def on_device(
    queries, key_rows, value_rows, residual, w_out, w_neck, w_first, w_second, w_class, labels
):
    encoded, loss, grad = block(
        queries.reshape(TOK, 128),
        key_rows.reshape(TOK, 128),
        value_rows.reshape(TOK, 128),
        labels.reshape(2, 32),
        w_out,
        residual.reshape(64, 1024),
        w_neck,
        w_first.reshape(27, 256, 256),
        w_second.reshape(27, 256, 256),
        w_class,
    )
    shape = residual.shape
    return (encoded.reshape(shape), loss.reshape(()), grad.reshape(shape))


def solution(mesh):
    slab = P("tok", None, None, "heads")
    rows = P("heads", "tok", None, None)
    placed = (slab, slab, slab, rows, P("heads", None), P(), P(), P(), P(), P("heads", None, "tok"))
    return jax.shard_map(
        on_device, mesh=mesh, in_specs=placed, out_specs=(rows, P(), rows), check_vma=False
    )
```

```python
import jax
import jax.numpy as jnp
from jax import lax
from jax.experimental import pallas as pl
from jax.experimental.pallas import tpu as pltpu
from jax.sharding import PartitionSpec as P

MESH = pl.DeviceIdType.MESH
BF = jnp.bfloat16
F32 = jnp.float32
HD = 64
LOSS_SCALE = 64.0
LOG2E = 1.4426950408889634
NN = (((1,), (0,)), ((), ()))
NT = (((1,), (1,)), ((), ()))
TOK = 512
ROWS = 528
NZ = 8
SLOT = {(0, 0): 0, (0, 1): 1}
for _k in (1, 2, 3):
    _b = 4 * _k - 2
    SLOT.update({(-_k, 0): _b, (_k, 0): _b + 1, (-_k, 1): _b + 2, (_k, 1): _b + 3})
SLOT.update({(4, 0): 14, (4, 1): 15})
DISTANCE = [None] * 16
for _key, _slot in SLOT.items():
    DISTANCE[_slot] = _key
TILES = [(0, 1), (2, 3, 4, 5), (6, 7, 8, 9), (10, 11, 12, 13), (14, 15)]


def place():
    heads, tok = lax.axis_index("heads"), lax.axis_index("tok")
    return heads, tok, tok // 4, (tok // 2) % 2, tok % 2


def at(heads, tok):
    return {"heads": heads, "tok": tok}


FAR, OWN, MATE = 0, 1, 2
NEAR = [(0, FAR), (1, FAR), (-1, FAR), (1, OWN), (-1, OWN), (1, MATE), (-1, MATE), (0, MATE)]
PARTS = ((0, TOK // 2), (TOK // 2, ROWS))


def block_kernel(
    q_hbm, k_hbm, v_hbm, lab_ref, w_hbm, res_hbm, neck_hbm, first_hbm, second_hbm, class_ref,
    enc_hbm, loss_ref, grad_hbm,
    kv, q_buf, qx, acc, peak, o_send, o_recv, lse_send, lse_recv, lab_send, lab_recv, attended,
    att_all, wf, neck, first, second, residual, result,
    halo_one, halo_two, halo_three, halo_four, grad_two, stat_a, stat_b, send_a, send_b,
    local_sem, kv_send, kv_recv, mate_send, y_send, y_recv, w_send, w_recv,
    a_send, a_recv, h_send, h_recv, s_send, s_recv, r_send, r_recv,
):
    heads, tok, z, y, core = place()
    up = at(heads, (tok + 4) % (4 * NZ))
    down = at(heads, (tok + 4 * NZ - 4) % (4 * NZ))
    mate = at(heads, tok + 1 - 2 * core)
    across = at(heads, tok + 2 - 4 * y)
    others = [at((heads + d) % 8, tok) for d in range(1, 8)]
    beside = {FAR: (tok + 31 + 2 * core) % 32, OWN: tok, MATE: tok + 1 - 2 * core}
    near = [at((heads + dh + 8) % 8, beside[plane]) for dh, plane in NEAR]
    group_a = [
        at((heads + d // 2) % 8, tok if d % 2 == 0 else tok + 1 - 2 * core) for d in range(1, 16)
    ]
    group_b = [
        at(heads, (tok + 4 * (d // 2)) % 32 if d % 2 == 0 else (tok + 4 * (d // 2) + 2 - 4 * y + 32) % 32)
        for d in range(1, 16)
    ]
    mine = pl.ds(pl.multiple_of(heads * 128, 128), 128)
    own_rows = pl.ds(pl.multiple_of(heads * 64, 64), 64)

    local = [
        pltpu.make_async_copy(k_hbm, kv.at[0, 0:TOK, 0:128], local_sem.at[0]),
        pltpu.make_async_copy(v_hbm, kv.at[0, 0:TOK, 128:256], local_sem.at[1]),
        pltpu.make_async_copy(q_hbm, q_buf.at[0], local_sem.at[2]),
        pltpu.make_async_copy(w_hbm, wf.at[mine], local_sem.at[3]),
    ]
    loads = [
        pltpu.make_async_copy(src, dst, local_sem.at[4 + i])
        for i, (src, dst) in enumerate(
            (
                (neck_hbm, neck),
                (first_hbm, first),
                (second_hbm, second),
                (res_hbm, residual),
            )
        )
    ]
    for copy in local:
        copy.start()
    barrier = pltpu.get_barrier_semaphore()
    peers = [up, down, mate, across] + others
    for peer in peers:
        pl.semaphore_signal(barrier, inc=1, device_id=peer, device_id_type=MESH)
    lab_rows = jnp.concatenate(
        [lab_ref[...].astype(F32), jnp.zeros((2, 224), F32)], axis=1
    )
    lab_rows = jnp.concatenate([lab_rows, jnp.zeros((14, 256), F32)], axis=0)
    kv[0, TOK:ROWS, :] = lab_rows.astype(BF)

    sent = []

    def send(src, dst, send_sem, recv_sem, peer):
        copy = pltpu.make_async_remote_copy(
            src_ref=src, dst_ref=dst, send_sem=send_sem, recv_sem=recv_sem, device_id=peer, device_id_type=MESH
        )
        copy.start()
        sent.append(copy)
        return copy

    arrivals = {}
    n_ring = [0]

    def ring(distance, part):
        slot = SLOT[(distance, 0)]
        lo, hi = PARTS[part]
        for step, peer in ((-1, up), (1, down)):
            if distance * step < 0:
                continue
            to = distance + step
            if abs(to) > 3:
                if part != (0 if step < 0 else 1):
                    continue
                to = 4
            dst = SLOT[(to, 0)]
            copy = send(
                kv.at[slot, lo:hi], kv.at[dst, lo:hi], kv_send.at[n_ring[0]], kv_recv.at[2 * dst + part], peer
            )
            n_ring[0] += 1
            arrivals[(to, 0, part)] = copy

    def share(distance, part):
        slot, dst = SLOT[(distance, 0)], SLOT[(distance, 1)]
        lo, hi = PARTS[part]
        arrivals[(distance, 1, part)] = send(
            kv.at[slot, lo:hi],
            kv.at[dst, lo:hi],
            mate_send.at[2 * slot + part],
            kv_recv.at[2 * dst + part],
            mate,
        )

    def arrive(k, part):
        for distance in (-k, k):
            arrivals[(distance, 0, part)].wait_recv()
            ring(distance, part)
            share(distance, part)

    def await_mate(*distances):
        for distance in distances:
            for part in range(2):
                arrivals[(distance, 1, part)].wait_recv()

    def prepare(half):
        lane = lax.broadcasted_iota(jnp.int32, (TOK, 128), 1)
        q = q_buf[half].astype(F32) * (HD**-0.5 * LOG2E)
        high = q.astype(BF)
        low = (q - high.astype(F32)).astype(BF)
        zero = jnp.zeros_like(high)
        rows = slice(half * TOK, (half + 1) * TOK)
        for h in range(2):
            mine_h = (lane < HD) if h == 0 else (lane >= HD)
            qx[h, rows, 0:128] = jnp.where(mine_h, high, zero)
            qx[h, rows, 128:256] = jnp.where(mine_h, low, zero)
        acc[rows] = jnp.zeros((TOK, 256), F32)
        peak[:, rows] = jnp.full((2, TOK, 128), -1e30, F32)

    def attend(half, slots):
        rows = slice(half * TOK, (half + 1) * TOK)
        lane = lax.broadcasted_iota(jnp.int32, (TOK, 128), 1)
        k = jnp.concatenate([kv[s, 0:TOK, 0:128] for s in slots], axis=0)
        kk = jnp.concatenate([k, k], axis=1)
        v = jnp.concatenate([kv[s, 0:TOK, 128:256] for s in slots], axis=0)
        vx = jnp.concatenate([v, jnp.ones_like(v)], axis=1)
        scores = [lax.dot_general(qx[h, rows, :], kk, NT, preferred_element_type=F32) for h in range(2)]
        sums, factors = [], []
        for h in range(2):
            old = peak[h, rows, :]
            new = jnp.maximum(old, jnp.max(scores[h], axis=1, keepdims=True))
            peak[h, rows, :] = new
            factors.append(jnp.exp2(old - new))
            mixing = jnp.exp2(scores[h] - new[:, :1]).astype(BF)
            sums.append(lax.dot_general(mixing, vx, NN, preferred_element_type=F32))
        factor = jnp.where(lane < HD, factors[0], factors[1])
        for part in (slice(0, 128), slice(128, 256)):
            acc[rows, part] = acc[rows, part] * factor + jnp.where(lane < HD, sums[0][:, part], sums[1][:, part])

    def finish(half):
        lane = lax.broadcasted_iota(jnp.int32, (TOK, 128), 1)
        rows = slice(half * TOK, (half + 1) * TOK)
        total = acc[rows, 128:256]
        top = jnp.where(lane < HD, peak[0, rows], peak[1, rows])
        return acc[rows, 0:128] / total, top + jnp.log(total) * LOG2E

    for copy in local:
        copy.wait()
    prepare(0)
    pl.semaphore_wait(barrier, len(peers))
    q_copy = send(q_buf.at[0], q_buf.at[1], y_send.at[0], y_recv.at[0], across)
    for part in range(2):
        ring(0, part)
    for part in range(2):
        share(0, part)
    w_copies = [send(wf.at[mine], wf.at[mine], w_send.at[d], w_recv.at[d], others[d]) for d in (3, 2, 4, 1, 5, 0, 6)]
    attend(0, (0,))
    await_mate(0)
    attend(0, (1,))
    for load in loads:
        load.start()
    q_copy.wait_recv()
    prepare(1)
    arrive(1, 0)
    attend(1, TILES[0])
    arrive(1, 1)
    attend(0, TILES[1][0:2])
    await_mate(-1, 1)
    attend(0, TILES[1][2:4])
    arrive(2, 0)
    arrive(2, 1)
    attend(1, TILES[1])
    await_mate(-2, 2)
    attend(0, TILES[2])
    arrive(3, 0)
    arrive(3, 1)
    attend(1, TILES[2])
    await_mate(-3, 3)
    for part in range(2):
        arrivals[(4, 0, part)].wait_recv()
        share(4, part)
    attend(1, TILES[3])
    await_mate(4)
    attend(1, TILES[4])

    part, lse = finish(1)
    o_send[...] = part.astype(BF)
    flat = lse.T
    row8 = lax.broadcasted_iota(jnp.int32, (8, TOK), 0)
    lse_send[...] = jnp.where(row8 < 4, jnp.broadcast_to(flat[0:1], (8, TOK)), jnp.broadcast_to(flat[64:65], (8, TOK)))
    label_rows = jnp.concatenate([kv[s, TOK:ROWS, :] for s in range(16)], axis=0)
    row = lax.broadcasted_iota(jnp.int32, (64, 256), 0)
    col = lax.broadcasted_iota(jnp.int32, (64, 256), 1)
    pick = jnp.zeros((64, 256), jnp.bool_)
    for s, (distance, other) in enumerate(DISTANCE):
        owner_core = core if other == 0 else 1 - core
        owner = ((z + distance + NZ) % NZ) * 4 + y * 2 + owner_core
        pick = pick | (((row % 32) == owner) & (col == 16 * s + row // 32))
    by_depth = lax.dot_general(
        jnp.where(pick, 1.0, 0.0).astype(BF), label_rows, NN, preferred_element_type=F32
    )

    def at_depth(depth):
        chosen = jnp.sum(jnp.where(col == depth, by_depth, 0.0), axis=1, keepdims=True)
        return jnp.broadcast_to(chosen, (64, 128))

    lab_send[...] = at_depth(tok + 2 - 4 * y).astype(BF)
    o_copy = send(o_send, o_recv, y_send.at[1], y_recv.at[1], across)
    lse_copy = send(lse_send, lse_recv, y_send.at[2], y_recv.at[2], across)
    lab_copy = send(lab_send, lab_recv, y_send.at[3], y_recv.at[3], across)
    attend(0, TILES[3])
    attend(0, TILES[4])
    own_part, my_lse = finish(0)
    lse_copy.wait_recv()
    head0 = jnp.broadcast_to(lse_recv[0:1], (64, TOK))
    head1 = jnp.broadcast_to(lse_recv[4:5], (64, TOK))
    its_lse = jnp.concatenate([head0, head1], axis=0).T
    top = jnp.maximum(my_lse, its_lse)
    my_share, its_share = jnp.exp2(my_lse - top), jnp.exp2(its_lse - top)
    both = my_share + its_share
    o_copy.wait_recv()
    merged = (my_share * own_part + its_share * o_recv[...].astype(F32)) / both
    attended[...] = merged.astype(BF)

    own = pltpu.make_async_copy(attended.at[own_rows], att_all.at[:, mine], local_sem.at[9])
    own.start()
    copies = []
    for i in range(7):
        theirs = lax.rem(heads + i + 1, 8)
        copies.append(
            send(
                attended.at[pl.ds(pl.multiple_of(theirs * 64, 64), 64)],
                att_all.at[:, mine],
                a_send.at[i],
                a_recv.at[i],
                others[i],
            )
        )
    lab_copy.wait_recv()
    labels = at_depth(tok) + lab_recv[...].astype(F32)

    def start_halo(stage, halo):
        halves = []
        for i, (dh, plane) in enumerate(NEAR):
            src, dst = {0: ((32, 96), (32, 96)), 1: ((64, 96), (0, 32)), -1: ((32, 64), (96, 128))}[dh]
            halves.append(
                send(
                    halo.at[OWN, src[0] : src[1]],
                    halo.at[plane, dst[0] : dst[1]],
                    h_send.at[stage, i],
                    h_recv.at[stage, i],
                    near[i],
                )
            )
        return halves

    def end_plane(halo, halves, plane):
        width = halo.shape[2]
        for copy, (_, its_plane) in zip(halves, NEAR):
            if its_plane == plane:
                copy.wait_recv()

        @pl.when(heads == 0)
        def _():
            halo[plane, 0:32] = jnp.zeros((32, width), BF)

        @pl.when(heads == 7)
        def _():
            halo[plane, 96:128] = jnp.zeros((32, width), BF)

        if plane == FAR:

            @pl.when((tok == 0) | (tok == 31))
            def _():
                halo[plane] = jnp.zeros((128, width), BF)

    def conv(halo, ready, weights, flipped):
        groups = halo.shape[2] // 256
        parts = [None] * 3
        for plane in (OWN, MATE, FAR):
            ready(plane)
            away = {OWN: 1, MATE: 2 - 2 * core, FAR: 2 * core}[plane]
            b = 2 - away if flipped else away
            for a in range(3):
                c = 2 - a if flipped else a
                window = [halo[plane, 32 * c : 32 * c + 64, 256 * g : 256 * g + 256] for g in range(groups)]
                window = jnp.concatenate(window, axis=0)
                for e in range(3):
                    term = lax.dot_general(
                        window, weights[(a * 3 + b) * 3 + e], NT if flipped else NN, preferred_element_type=F32
                    )
                    parts[e] = term if parts[e] is None else parts[e] + term
        if flipped:
            parts = parts[::-1]
        rows = 64 * groups
        inline = lax.broadcasted_iota(jnp.int32, (rows, 256), 0) % 32
        before = jnp.where(inline == 0, 0.0, pltpu.roll(parts[0], 1, 0))
        after = jnp.where(inline == 31, 0.0, pltpu.roll(parts[2], rows - 1, 0))
        return before + parts[1] + after

    def sigmoid(v):
        return 1.0 / (1.0 + jnp.exp(-v))

    for load in loads:
        load.wait()
    for copy in w_copies:
        copy.wait_recv()
    own.wait()
    for copy in copies:
        copy.wait_recv()
    projected = lax.dot_general(att_all[...], wf[...], NN, preferred_element_type=F32)
    encoded = (residual[...].astype(F32) + projected).astype(BF)
    halo_one[1, 32:96] = lax.dot_general(encoded, neck[...], NN, preferred_element_type=F32).astype(BF)
    halves_one = start_halo(0, halo_one)
    result[0] = encoded
    enc_copy = pltpu.make_async_copy(result.at[0], enc_hbm, local_sem.at[10])
    enc_copy.start()
    hidden_one = conv(halo_one, lambda plane: end_plane(halo_one, halves_one, plane), first, False)
    gate_one = sigmoid(hidden_one)
    halo_two[1, 32:96] = (hidden_one * gate_one).astype(BF)
    halves_two = start_halo(1, halo_two)
    slope_one = gate_one * (1.0 + hidden_one * (1.0 - gate_one))
    hidden_two = conv(halo_two, lambda plane: end_plane(halo_two, halves_two, plane), second, False)
    gate_two = sigmoid(hidden_two)
    active_two = (hidden_two * gate_two).astype(BF).astype(F32)
    w_class = class_ref[...].reshape(1, 256).astype(F32)
    logits = jnp.sum(active_two * w_class, axis=1, keepdims=True)
    probability = jnp.broadcast_to(sigmoid(logits), (64, 128))
    spread = probability * (1.0 - probability)
    slope_two = gate_two * (1.0 + hidden_two * (1.0 - gate_two))
    unscaled = jnp.concatenate([spread, spread], axis=1) * w_class * slope_two
    halo_three[1, 32:96, 0:256] = unscaled.astype(BF)
    halo_three[1, 32:96, 256:384] = labels.astype(BF)
    halves_three = start_halo(2, halo_three)

    def over_cells(value):
        return jnp.sum(value, axis=0, keepdims=True)

    row8 = lax.broadcasted_iota(jnp.int32, (8, 128), 0)
    stats = jnp.where(
        row8 == 0,
        over_cells(probability * labels),
        jnp.where(row8 == 1, over_cells(probability), over_cells(labels)),
    )
    index_a = heads * 2 + core
    send_a[...] = stats
    stat_copies = [
        send(send_a, stat_a.at[index_a], s_send.at[d], s_recv.at[d], group_a[d]) for d in range(15)
    ]
    stat_a[index_a] = stats
    index_b = z * 2 + y

    def split_kinds(plane):
        end_plane(halo_three, halves_three, plane)
        cells = halo_three[plane, :, 256:384]
        cells = jnp.concatenate([cells, cells], axis=1).astype(F32)
        slopes = halo_three[plane, :, 0:256].astype(F32)
        grad_two[plane, :, 0:256] = (slopes * cells).astype(BF)
        grad_two[plane, :, 256:512] = (slopes * (1.0 - cells)).astype(BF)

    grad_active = conv(grad_two, split_kinds, second, True)
    halo_four[1, 32:96, 0:256] = (grad_active[0:64] * slope_one).astype(BF)
    halo_four[1, 32:96, 256:512] = (grad_active[64:128] * slope_one).astype(BF)
    halves_four = start_halo(3, halo_four)
    for copy in stat_copies:
        copy.wait_recv()
    partial = stat_a[0]
    for i in range(1, 16):
        partial = partial + stat_a[i]
    send_b[...] = partial
    total_copies = [
        send(send_b, stat_b.at[index_b], r_send.at[d], r_recv.at[d], group_b[d]) for d in range(15)
    ]
    stat_b[index_b] = partial
    by_kind = conv(halo_four, lambda plane: end_plane(halo_four, halves_four, plane), first, True)
    for copy in total_copies:
        copy.wait_recv()
    sums = stat_b[0]
    for i in range(1, 16):
        sums = sums + stat_b[i]
    intersection, denominator = sums[0:1], sums[1:2] + sums[2:3]
    loss_ref[0, 0] = (1.0 - 2.0 * intersection / denominator)[0, 0]
    scale = LOSS_SCALE * 16384.0 * -2.0 / (denominator * denominator)
    fault, rest = scale * (denominator - intersection), scale * -intersection
    fault, rest = jnp.concatenate([fault, fault], axis=1), jnp.concatenate([rest, rest], axis=1)
    grad_neck = (by_kind[0:64] * fault + by_kind[64:128] * rest).astype(BF)
    result[1] = lax.dot_general(grad_neck, neck[...], NT, preferred_element_type=F32).astype(BF)
    grad_copy = pltpu.make_async_copy(result.at[1], grad_hbm, local_sem.at[11])
    grad_copy.start()
    enc_copy.wait()
    for copy in sent:
        copy.wait_send()
    grad_copy.wait()


def block(queries, key_rows, value_rows, labels, w_out, residual, w_neck, w_first, w_second, w_class):
    dma = pltpu.SemaphoreType.DMA
    vmem, anywhere = pl.BlockSpec(memory_space=pltpu.VMEM), pl.BlockSpec(memory_space=pl.ANY)
    return pl.pallas_call(
        block_kernel,
        out_shape=(
            jax.ShapeDtypeStruct((64, 1024), BF),
            jax.ShapeDtypeStruct((1, 1), F32),
            jax.ShapeDtypeStruct((64, 1024), BF),
        ),
        in_specs=[anywhere] * 3 + [vmem] + [anywhere] * 5 + [vmem],
        out_specs=(anywhere, pl.BlockSpec(memory_space=pltpu.SMEM), anywhere),
        scratch_shapes=[
            pltpu.VMEM((16, ROWS, 256), BF),
            pltpu.VMEM((2, TOK, 128), BF),
            pltpu.VMEM((2, 2 * TOK, 256), BF),
            pltpu.VMEM((2 * TOK, 256), F32),
            pltpu.VMEM((2, 2 * TOK, 128), F32),
            pltpu.VMEM((TOK, 128), BF),
            pltpu.VMEM((TOK, 128), BF),
            pltpu.VMEM((8, TOK), F32),
            pltpu.VMEM((8, TOK), F32),
            pltpu.VMEM((64, 128), BF),
            pltpu.VMEM((64, 128), BF),
            pltpu.VMEM((TOK, 128), BF),
            pltpu.VMEM((64, 1024), BF),
            pltpu.VMEM((1024, 1024), BF),
            pltpu.VMEM((1024, 256), BF),
            pltpu.VMEM((27, 256, 256), BF),
            pltpu.VMEM((27, 256, 256), BF),
            pltpu.VMEM((64, 1024), BF),
            pltpu.VMEM((2, 64, 1024), BF),
            pltpu.VMEM((3, 128, 256), BF),
            pltpu.VMEM((3, 128, 256), BF),
            pltpu.VMEM((3, 128, 384), BF),
            pltpu.VMEM((3, 128, 512), BF),
            pltpu.VMEM((3, 128, 512), BF),
            pltpu.VMEM((16, 8, 128), F32),
            pltpu.VMEM((16, 8, 128), F32),
            pltpu.VMEM((8, 128), F32),
            pltpu.VMEM((8, 128), F32),
            dma((12,)),
            dma((16,)),
            dma((32,)),
            dma((32,)),
            dma((4,)),
            dma((4,)),
            dma((7,)),
            dma((7,)),
            dma((7,)),
            dma((7,)),
            dma((4, 8)),
            dma((4, 8)),
            dma((15,)),
            dma((15,)),
            dma((15,)),
            dma((15,)),
        ],
        compiler_params=pltpu.CompilerParams(
            collective_id=0, has_side_effects=True, vmem_limit_bytes=67043328
        ),
        name="block",
    )(queries, key_rows, value_rows, labels, w_out, residual, w_neck, w_first, w_second, w_class)


def on_device(
    queries, key_rows, value_rows, residual, w_out, w_neck, w_first, w_second, w_class, labels
):
    encoded, loss, grad = block(
        queries.reshape(TOK, 128),
        key_rows.reshape(TOK, 128),
        value_rows.reshape(TOK, 128),
        labels.reshape(2, 32),
        w_out,
        residual.reshape(64, 1024),
        w_neck,
        w_first.reshape(27, 256, 256),
        w_second.reshape(27, 256, 256),
        w_class,
    )
    shape = residual.shape
    return (encoded.reshape(shape), loss.reshape(()), grad.reshape(shape))


def solution(mesh):
    slab = P("tok", None, None, "heads")
    rows = P("heads", "tok", None, None)
    placed = (slab, slab, slab, rows, P("heads", None), P(), P(), P(), P(), P("heads", None, "tok"))
    return jax.shard_map(
        on_device, mesh=mesh, in_specs=placed, out_specs=(rows, P(), rows), check_vma=False
    )
```

```python
import jax
import jax.numpy as jnp
from jax import lax
from jax.experimental import pallas as pl
from jax.experimental.pallas import tpu as pltpu
from jax.sharding import PartitionSpec as P

MESH = pl.DeviceIdType.MESH
BF = jnp.bfloat16
F32 = jnp.float32
HD = 64
LOSS_SCALE = 64.0
LOG2E = 1.4426950408889634
NN = (((1,), (0,)), ((), ()))
NT = (((1,), (1,)), ((), ()))
TOK = 512
ROWS = 528
NZ = 8
SLOT = {(0, 0): 0, (0, 1): 1}
for _k in (1, 2, 3):
    _b = 4 * _k - 2
    SLOT.update({(-_k, 0): _b, (_k, 0): _b + 1, (-_k, 1): _b + 2, (_k, 1): _b + 3})
SLOT.update({(4, 0): 14, (4, 1): 15})
DISTANCE = [None] * 16
for _key, _slot in SLOT.items():
    DISTANCE[_slot] = _key
TILES = [(0, 1), (2, 3, 4, 5), (6, 7, 8, 9), (10, 11, 12, 13), (14, 15)]


def place():
    heads, tok = lax.axis_index("heads"), lax.axis_index("tok")
    return heads, tok, tok // 4, (tok // 2) % 2, tok % 2


def at(heads, tok):
    return {"heads": heads, "tok": tok}


FAR, OWN, MATE = 0, 1, 2
NEAR = [(0, FAR), (1, FAR), (-1, FAR), (1, OWN), (-1, OWN), (1, MATE), (-1, MATE), (0, MATE)]
PARTS = ((0, TOK // 2), (TOK // 2, ROWS))


def block_kernel(
    q_hbm, k_hbm, v_hbm, lab_ref, w_hbm, res_hbm, neck_hbm, first_hbm, second_hbm, class_ref,
    enc_ref, loss_ref, grad_ref,
    kv, q_buf, qx, acc, peak, o_send, o_recv, lse_send, lse_recv, lab_send, lab_recv, attended,
    att_all, wf, neck, first, second, residual,
    halo_one, halo_two, halo_three, halo_four, grad_two, stat_a, stat_b, send_a, send_b,
    local_sem, kv_send, kv_recv, mate_send, y_send, y_recv, w_send, w_recv,
    a_send, a_recv, h_send, h_recv, s_send, s_recv, r_send, r_recv,
):
    heads, tok, z, y, core = place()
    up = at(heads, (tok + 4) % (4 * NZ))
    down = at(heads, (tok + 4 * NZ - 4) % (4 * NZ))
    mate = at(heads, tok + 1 - 2 * core)
    across = at(heads, tok + 2 - 4 * y)
    others = [at((heads + d) % 8, tok) for d in range(1, 8)]
    beside = {FAR: (tok + 31 + 2 * core) % 32, OWN: tok, MATE: tok + 1 - 2 * core}
    near = [at((heads + dh + 8) % 8, beside[plane]) for dh, plane in NEAR]
    group_a = [
        at((heads + d // 2) % 8, tok if d % 2 == 0 else tok + 1 - 2 * core) for d in range(1, 16)
    ]
    group_b = [
        at(heads, (tok + 4 * (d // 2)) % 32 if d % 2 == 0 else (tok + 4 * (d // 2) + 2 - 4 * y + 32) % 32)
        for d in range(1, 16)
    ]
    mine = pl.ds(pl.multiple_of(heads * 128, 128), 128)
    own_rows = pl.ds(pl.multiple_of(heads * 64, 64), 64)

    local = [
        pltpu.make_async_copy(k_hbm, kv.at[0, 0:TOK, 0:128], local_sem.at[0]),
        pltpu.make_async_copy(v_hbm, kv.at[0, 0:TOK, 128:256], local_sem.at[1]),
        pltpu.make_async_copy(q_hbm, q_buf.at[0], local_sem.at[2]),
        pltpu.make_async_copy(w_hbm, wf.at[mine], local_sem.at[3]),
    ]
    loads = [
        pltpu.make_async_copy(src, dst, local_sem.at[4 + i])
        for i, (src, dst) in enumerate(
            (
                (neck_hbm, neck),
                (first_hbm, first),
                (second_hbm, second),
                (res_hbm, residual),
            )
        )
    ]
    for copy in local:
        copy.start()
    barrier = pltpu.get_barrier_semaphore()
    peers = [up, down, mate, across] + others
    for peer in peers:
        pl.semaphore_signal(barrier, inc=1, device_id=peer, device_id_type=MESH)
    lab_rows = jnp.concatenate(
        [lab_ref[...].astype(F32), jnp.zeros((2, 224), F32)], axis=1
    )
    lab_rows = jnp.concatenate([lab_rows, jnp.zeros((14, 256), F32)], axis=0)
    kv[0, TOK:ROWS, :] = lab_rows.astype(BF)

    sent = []

    def send(src, dst, send_sem, recv_sem, peer):
        copy = pltpu.make_async_remote_copy(
            src_ref=src, dst_ref=dst, send_sem=send_sem, recv_sem=recv_sem, device_id=peer, device_id_type=MESH
        )
        copy.start()
        sent.append(copy)
        return copy

    arrivals = {}
    n_ring = [0]

    def ring(distance, part):
        slot = SLOT[(distance, 0)]
        lo, hi = PARTS[part]
        for step, peer in ((-1, up), (1, down)):
            if distance * step < 0:
                continue
            to = distance + step
            if abs(to) > 3:
                if part != (0 if step < 0 else 1):
                    continue
                to = 4
            dst = SLOT[(to, 0)]
            copy = send(
                kv.at[slot, lo:hi], kv.at[dst, lo:hi], kv_send.at[n_ring[0]], kv_recv.at[2 * dst + part], peer
            )
            n_ring[0] += 1
            arrivals[(to, 0, part)] = copy

    def share(distance, part):
        slot, dst = SLOT[(distance, 0)], SLOT[(distance, 1)]
        lo, hi = PARTS[part]
        arrivals[(distance, 1, part)] = send(
            kv.at[slot, lo:hi],
            kv.at[dst, lo:hi],
            mate_send.at[2 * slot + part],
            kv_recv.at[2 * dst + part],
            mate,
        )

    def arrive(k, part):
        for distance in (-k, k):
            arrivals[(distance, 0, part)].wait_recv()
            ring(distance, part)
            share(distance, part)

    def await_mate(*distances):
        for distance in distances:
            for part in range(2):
                arrivals[(distance, 1, part)].wait_recv()

    def prepare(half):
        lane = lax.broadcasted_iota(jnp.int32, (TOK, 128), 1)
        q = q_buf[half].astype(F32) * (HD**-0.5 * LOG2E)
        high = q.astype(BF)
        low = (q - high.astype(F32)).astype(BF)
        zero = jnp.zeros_like(high)
        rows = slice(half * TOK, (half + 1) * TOK)
        for h in range(2):
            mine_h = (lane < HD) if h == 0 else (lane >= HD)
            qx[h, rows, 0:128] = jnp.where(mine_h, high, zero)
            qx[h, rows, 128:256] = jnp.where(mine_h, low, zero)
        acc[rows] = jnp.zeros((TOK, 256), F32)
        peak[:, rows] = jnp.full((2, TOK, 128), -1e30, F32)

    def attend(half, slots):
        rows = slice(half * TOK, (half + 1) * TOK)
        lane = lax.broadcasted_iota(jnp.int32, (TOK, 128), 1)
        k = jnp.concatenate([kv[s, 0:TOK, 0:128] for s in slots], axis=0)
        kk = jnp.concatenate([k, k], axis=1)
        v = jnp.concatenate([kv[s, 0:TOK, 128:256] for s in slots], axis=0)
        vx = jnp.concatenate([v, jnp.ones_like(v)], axis=1)
        scores = [lax.dot_general(qx[h, rows, :], kk, NT, preferred_element_type=F32) for h in range(2)]
        sums, factors = [], []
        for h in range(2):
            old = peak[h, rows, :]
            new = jnp.maximum(old, jnp.max(scores[h], axis=1, keepdims=True))
            peak[h, rows, :] = new
            factors.append(jnp.exp2(old - new))
            mixing = jnp.exp2(scores[h] - new[:, :1]).astype(BF)
            sums.append(lax.dot_general(mixing, vx, NN, preferred_element_type=F32))
        factor = jnp.where(lane < HD, factors[0], factors[1])
        for part in (slice(0, 128), slice(128, 256)):
            acc[rows, part] = acc[rows, part] * factor + jnp.where(lane < HD, sums[0][:, part], sums[1][:, part])

    def finish(half):
        lane = lax.broadcasted_iota(jnp.int32, (TOK, 128), 1)
        rows = slice(half * TOK, (half + 1) * TOK)
        total = acc[rows, 128:256]
        top = jnp.where(lane < HD, peak[0, rows], peak[1, rows])
        return acc[rows, 0:128] / total, top + jnp.log(total) * LOG2E

    for copy in local:
        copy.wait()
    prepare(0)
    pl.semaphore_wait(barrier, len(peers))
    q_copy = send(q_buf.at[0], q_buf.at[1], y_send.at[0], y_recv.at[0], across)
    for part in range(2):
        ring(0, part)
    for part in range(2):
        share(0, part)
    w_copies = [send(wf.at[mine], wf.at[mine], w_send.at[d], w_recv.at[d], others[d]) for d in (3, 2, 4, 1, 5, 0, 6)]
    attend(0, (0,))
    await_mate(0)
    attend(0, (1,))
    for load in loads:
        load.start()
    q_copy.wait_recv()
    prepare(1)
    arrive(1, 0)
    attend(1, TILES[0])
    arrive(1, 1)
    attend(0, TILES[1][0:2])
    await_mate(-1, 1)
    attend(0, TILES[1][2:4])
    arrive(2, 0)
    arrive(2, 1)
    attend(1, TILES[1])
    await_mate(-2, 2)
    attend(0, TILES[2])
    arrive(3, 0)
    arrive(3, 1)
    attend(1, TILES[2])
    await_mate(-3, 3)
    for part in range(2):
        arrivals[(4, 0, part)].wait_recv()
        share(4, part)
    attend(1, TILES[3])
    await_mate(4)
    attend(1, TILES[4])

    part, lse = finish(1)
    o_send[...] = part.astype(BF)
    flat = lse.T
    row8 = lax.broadcasted_iota(jnp.int32, (8, TOK), 0)
    lse_send[...] = jnp.where(row8 < 4, jnp.broadcast_to(flat[0:1], (8, TOK)), jnp.broadcast_to(flat[64:65], (8, TOK)))
    label_rows = jnp.concatenate([kv[s, TOK:ROWS, :] for s in range(16)], axis=0)
    row = lax.broadcasted_iota(jnp.int32, (64, 256), 0)
    col = lax.broadcasted_iota(jnp.int32, (64, 256), 1)
    pick = jnp.zeros((64, 256), jnp.bool_)
    for s, (distance, other) in enumerate(DISTANCE):
        owner_core = core if other == 0 else 1 - core
        owner = ((z + distance + NZ) % NZ) * 4 + y * 2 + owner_core
        pick = pick | (((row % 32) == owner) & (col == 16 * s + row // 32))
    by_depth = lax.dot_general(
        jnp.where(pick, 1.0, 0.0).astype(BF), label_rows, NN, preferred_element_type=F32
    )

    def at_depth(depth):
        chosen = jnp.sum(jnp.where(col == depth, by_depth, 0.0), axis=1, keepdims=True)
        return jnp.broadcast_to(chosen, (64, 128))

    lab_send[...] = at_depth(tok + 2 - 4 * y).astype(BF)
    o_copy = send(o_send, o_recv, y_send.at[1], y_recv.at[1], across)
    lse_copy = send(lse_send, lse_recv, y_send.at[2], y_recv.at[2], across)
    lab_copy = send(lab_send, lab_recv, y_send.at[3], y_recv.at[3], across)
    attend(0, TILES[3])
    attend(0, TILES[4])
    own_part, my_lse = finish(0)
    lse_copy.wait_recv()
    head0 = jnp.broadcast_to(lse_recv[0:1], (64, TOK))
    head1 = jnp.broadcast_to(lse_recv[4:5], (64, TOK))
    its_lse = jnp.concatenate([head0, head1], axis=0).T
    top = jnp.maximum(my_lse, its_lse)
    my_share, its_share = jnp.exp2(my_lse - top), jnp.exp2(its_lse - top)
    both = my_share + its_share
    o_copy.wait_recv()
    merged = (my_share * own_part + its_share * o_recv[...].astype(F32)) / both
    attended[...] = merged.astype(BF)

    own = pltpu.make_async_copy(attended.at[own_rows], att_all.at[:, mine], local_sem.at[9])
    own.start()
    copies = []
    for i in range(7):
        theirs = lax.rem(heads + i + 1, 8)
        copies.append(
            send(
                attended.at[pl.ds(pl.multiple_of(theirs * 64, 64), 64)],
                att_all.at[:, mine],
                a_send.at[i],
                a_recv.at[i],
                others[i],
            )
        )
    lab_copy.wait_recv()
    labels = at_depth(tok) + lab_recv[...].astype(F32)

    def start_halo(stage, halo):
        halves = []
        for i, (dh, plane) in enumerate(NEAR):
            src, dst = {0: ((32, 96), (32, 96)), 1: ((64, 96), (0, 32)), -1: ((32, 64), (96, 128))}[dh]
            halves.append(
                send(
                    halo.at[OWN, src[0] : src[1]],
                    halo.at[plane, dst[0] : dst[1]],
                    h_send.at[stage, i],
                    h_recv.at[stage, i],
                    near[i],
                )
            )
        return halves

    def end_plane(halo, halves, plane):
        width = halo.shape[2]
        for copy, (_, its_plane) in zip(halves, NEAR):
            if its_plane == plane:
                copy.wait_recv()

        @pl.when(heads == 0)
        def _():
            halo[plane, 0:32] = jnp.zeros((32, width), BF)

        @pl.when(heads == 7)
        def _():
            halo[plane, 96:128] = jnp.zeros((32, width), BF)

        if plane == FAR:

            @pl.when((tok == 0) | (tok == 31))
            def _():
                halo[plane] = jnp.zeros((128, width), BF)

    def conv(halo, ready, weights, flipped):
        groups = halo.shape[2] // 256
        parts = [None] * 3
        for plane in (OWN, MATE, FAR):
            ready(plane)
            away = {OWN: 1, MATE: 2 - 2 * core, FAR: 2 * core}[plane]
            b = 2 - away if flipped else away
            for a in range(3):
                c = 2 - a if flipped else a
                window = [halo[plane, 32 * c : 32 * c + 64, 256 * g : 256 * g + 256] for g in range(groups)]
                window = jnp.concatenate(window, axis=0)
                for e in range(3):
                    term = lax.dot_general(
                        window, weights[(a * 3 + b) * 3 + e], NT if flipped else NN, preferred_element_type=F32
                    )
                    parts[e] = term if parts[e] is None else parts[e] + term
        if flipped:
            parts = parts[::-1]
        rows = 64 * groups
        inline = lax.broadcasted_iota(jnp.int32, (rows, 256), 0) % 32
        before = jnp.where(inline == 0, 0.0, pltpu.roll(parts[0], 1, 0))
        after = jnp.where(inline == 31, 0.0, pltpu.roll(parts[2], rows - 1, 0))
        return before + parts[1] + after

    def sigmoid(v):
        return 1.0 / (1.0 + jnp.exp(-v))

    for load in loads:
        load.wait()
    for copy in w_copies:
        copy.wait_recv()
    own.wait()
    for copy in copies:
        copy.wait_recv()
    projected = lax.dot_general(att_all[...], wf[...], NN, preferred_element_type=F32)
    encoded = (residual[...].astype(F32) + projected).astype(BF)
    halo_one[1, 32:96] = lax.dot_general(encoded, neck[...], NN, preferred_element_type=F32).astype(BF)
    halves_one = start_halo(0, halo_one)
    enc_ref[...] = encoded
    hidden_one = conv(halo_one, lambda plane: end_plane(halo_one, halves_one, plane), first, False)
    gate_one = sigmoid(hidden_one)
    halo_two[1, 32:96] = (hidden_one * gate_one).astype(BF)
    halves_two = start_halo(1, halo_two)
    slope_one = gate_one * (1.0 + hidden_one * (1.0 - gate_one))
    hidden_two = conv(halo_two, lambda plane: end_plane(halo_two, halves_two, plane), second, False)
    gate_two = sigmoid(hidden_two)
    active_two = (hidden_two * gate_two).astype(BF).astype(F32)
    w_class = class_ref[...].reshape(1, 256).astype(F32)
    logits = jnp.sum(active_two * w_class, axis=1, keepdims=True)
    probability = jnp.broadcast_to(sigmoid(logits), (64, 128))
    spread = probability * (1.0 - probability)
    slope_two = gate_two * (1.0 + hidden_two * (1.0 - gate_two))
    unscaled = jnp.concatenate([spread, spread], axis=1) * w_class * slope_two
    halo_three[1, 32:96, 0:256] = unscaled.astype(BF)
    halo_three[1, 32:96, 256:384] = labels.astype(BF)
    halves_three = start_halo(2, halo_three)

    def over_cells(value):
        return jnp.sum(value, axis=0, keepdims=True)

    row8 = lax.broadcasted_iota(jnp.int32, (8, 128), 0)
    stats = jnp.where(
        row8 == 0,
        over_cells(probability * labels),
        jnp.where(row8 == 1, over_cells(probability), over_cells(labels)),
    )
    index_a = heads * 2 + core
    send_a[...] = stats
    stat_copies = [
        send(send_a, stat_a.at[index_a], s_send.at[d], s_recv.at[d], group_a[d]) for d in range(15)
    ]
    stat_a[index_a] = stats
    index_b = z * 2 + y

    def split_kinds(plane):
        end_plane(halo_three, halves_three, plane)
        cells = halo_three[plane, :, 256:384]
        cells = jnp.concatenate([cells, cells], axis=1).astype(F32)
        slopes = halo_three[plane, :, 0:256].astype(F32)
        grad_two[plane, :, 0:256] = (slopes * cells).astype(BF)
        grad_two[plane, :, 256:512] = (slopes * (1.0 - cells)).astype(BF)

    grad_active = conv(grad_two, split_kinds, second, True)
    halo_four[1, 32:96, 0:256] = (grad_active[0:64] * slope_one).astype(BF)
    halo_four[1, 32:96, 256:512] = (grad_active[64:128] * slope_one).astype(BF)
    halves_four = start_halo(3, halo_four)
    for copy in stat_copies:
        copy.wait_recv()
    partial = stat_a[0]
    for i in range(1, 16):
        partial = partial + stat_a[i]
    send_b[...] = partial
    total_copies = [
        send(send_b, stat_b.at[index_b], r_send.at[d], r_recv.at[d], group_b[d]) for d in range(15)
    ]
    stat_b[index_b] = partial
    by_kind = conv(halo_four, lambda plane: end_plane(halo_four, halves_four, plane), first, True)
    for copy in total_copies:
        copy.wait_recv()
    sums = stat_b[0]
    for i in range(1, 16):
        sums = sums + stat_b[i]
    intersection, denominator = sums[0:1], sums[1:2] + sums[2:3]
    loss_ref[0, 0] = (1.0 - 2.0 * intersection / denominator)[0, 0]
    scale = LOSS_SCALE * 16384.0 * -2.0 / (denominator * denominator)
    fault, rest = scale * (denominator - intersection), scale * -intersection
    fault, rest = jnp.concatenate([fault, fault], axis=1), jnp.concatenate([rest, rest], axis=1)
    grad_neck = (by_kind[0:64] * fault + by_kind[64:128] * rest).astype(BF)
    grad_ref[...] = lax.dot_general(grad_neck, neck[...], NT, preferred_element_type=F32).astype(BF)
    for copy in sent:
        copy.wait_send()


def block(queries, key_rows, value_rows, labels, w_out, residual, w_neck, w_first, w_second, w_class):
    dma = pltpu.SemaphoreType.DMA
    vmem, anywhere = pl.BlockSpec(memory_space=pltpu.VMEM), pl.BlockSpec(memory_space=pl.ANY)
    return pl.pallas_call(
        block_kernel,
        out_shape=(
            jax.ShapeDtypeStruct((64, 1024), BF),
            jax.ShapeDtypeStruct((1, 1), F32),
            jax.ShapeDtypeStruct((64, 1024), BF),
        ),
        in_specs=[anywhere] * 3 + [vmem] + [anywhere] * 5 + [vmem],
        out_specs=(vmem, pl.BlockSpec(memory_space=pltpu.SMEM), vmem),
        scratch_shapes=[
            pltpu.VMEM((16, ROWS, 256), BF),
            pltpu.VMEM((2, TOK, 128), BF),
            pltpu.VMEM((2, 2 * TOK, 256), BF),
            pltpu.VMEM((2 * TOK, 256), F32),
            pltpu.VMEM((2, 2 * TOK, 128), F32),
            pltpu.VMEM((TOK, 128), BF),
            pltpu.VMEM((TOK, 128), BF),
            pltpu.VMEM((8, TOK), F32),
            pltpu.VMEM((8, TOK), F32),
            pltpu.VMEM((64, 128), BF),
            pltpu.VMEM((64, 128), BF),
            pltpu.VMEM((TOK, 128), BF),
            pltpu.VMEM((64, 1024), BF),
            pltpu.VMEM((1024, 1024), BF),
            pltpu.VMEM((1024, 256), BF),
            pltpu.VMEM((27, 256, 256), BF),
            pltpu.VMEM((27, 256, 256), BF),
            pltpu.VMEM((64, 1024), BF),
            pltpu.VMEM((3, 128, 256), BF),
            pltpu.VMEM((3, 128, 256), BF),
            pltpu.VMEM((3, 128, 384), BF),
            pltpu.VMEM((3, 128, 512), BF),
            pltpu.VMEM((3, 128, 512), BF),
            pltpu.VMEM((16, 8, 128), F32),
            pltpu.VMEM((16, 8, 128), F32),
            pltpu.VMEM((8, 128), F32),
            pltpu.VMEM((8, 128), F32),
            dma((10,)),
            dma((16,)),
            dma((32,)),
            dma((32,)),
            dma((4,)),
            dma((4,)),
            dma((7,)),
            dma((7,)),
            dma((7,)),
            dma((7,)),
            dma((4, 8)),
            dma((4, 8)),
            dma((15,)),
            dma((15,)),
            dma((15,)),
            dma((15,)),
        ],
        compiler_params=pltpu.CompilerParams(
            collective_id=0, has_side_effects=True, vmem_limit_bytes=48 << 20
        ),
        name="block",
    )(queries, key_rows, value_rows, labels, w_out, residual, w_neck, w_first, w_second, w_class)


def on_device(
    queries, key_rows, value_rows, residual, w_out, w_neck, w_first, w_second, w_class, labels
):
    operands = (
        queries.reshape(TOK, 128),
        key_rows.reshape(TOK, 128),
        value_rows.reshape(TOK, 128),
        labels.reshape(2, 32),
        w_out,
        residual.reshape(64, 1024),
        w_neck,
        w_first.reshape(27, 256, 256),
        w_second.reshape(27, 256, 256),
        w_class,
    )
    encoded, loss, grad = block(*(pltpu.with_memory_space_constraint(operand, pltpu.HBM) for operand in operands))
    shape = residual.shape
    return (encoded.reshape(shape), loss.reshape(()), grad.reshape(shape))


def solution(mesh):
    slab = P("tok", None, None, "heads")
    rows = P("heads", "tok", None, None)
    placed = (slab, slab, slab, rows, P("heads", None), P(), P(), P(), P(), P("heads", None, "tok"))
    return jax.shard_map(
        on_device, mesh=mesh, in_specs=placed, out_specs=(rows, P(), rows), check_vma=False
    )
```
